128 devices in a mesh: sub: 16 (over x, y), rep: 8 (over z, core).
Axes of the slice: x: 4, y: 4, z: 4, core: 2. Of those that a mesh axis runs over, the one named last changes fastest.
Arguments:
- rhs: float32 [4096, 128], P('sub'), may hold values from -31 to 31
- schur_diag: bfloat16 [4096, 256], P('sub'), may hold values from -0.375 to 0.375
- precond: bfloat16 [4096, 512], P('sub'), may hold values from -0.25 to 0.25
- halo_ids: int32 [16, 2], P('sub'), may hold values from 0 to 31, as said below
- factors: bfloat16 [256, 1024, 1024], P(('sub', 'rep')), may hold values from -0.1875 to 0.1875
- couplings: bfloat16 [256, 1024, 512], P(('sub', 'rep')), may hold values from -0.09375 to 0.09375
- block_ids: int32 [256, 4], P(('sub', 'rep')), may hold values from 0 to 31
- counts: int32 [128], P(('sub', 'rep')), may hold values from 1 to 2, 160 in all
Outputs:
- solution: float32 [4096, 128], P('sub')
The draws below stay inside these ranges and needn't reach their ends.
Inputs may be any that keep to these rules, and one draw needn't show every extreme that they name: `halo_ids`: in row d the first 1 entries name blocks owned by index d - 1 of sub and the others blocks owned by index d + 1, cyclically; block b is owned by index b // 2. counts[i] belongs to device i of sub+rep, sub slowest; slots k with k % 2 >= counts[k // 2] are not part of the operator.
All inputs are finite; a program needn't handle non-finite values.
Results may differ from the reference program's by a relative error of at most 0.0031.
Values may be sent and summed in bfloat16 or wider, within the bound.
No kernel may reach another device: no remote copies, remote signals or barrier semaphores. Data moves between devices by JAX's collectives and lax.ppermute only.
A program may use at most 64 MiB of HBM per device.

```python
import math
import jax
import jax.numpy as jnp
import numpy as np
from jax import lax

BLK = 1024
BI = 128
IFB = 4
HB = 2
NRHS = 128
NB_DEV = 2
GB_DEV = 2
GBLK = 32
G = 4096
EXT = 512
SLOTS = 256
N_SUB = 16
DEVICES = 128


def draw_rhs(key, part):
    key_scale, key_base = jax.random.split(jax.random.fold_in(key, 11), 2)
    scales = jnp.exp(jax.random.uniform(key_scale, (G, 1), minval=0.0, maxval=math.log(10.0)))
    rising = 1.0 + 2.0 * jnp.arange(G, dtype=jnp.float32)[:, None] / G
    base = jnp.clip(jax.random.normal(key_base, (G, NRHS)), -6.0, 6.0)
    return (base * scales * rising / 6.0).astype(jnp.float32)


def draw_halo_ids(key, part):
    owners_row = jnp.arange(N_SUB, dtype=jnp.int32)[:, None]
    left_side = jnp.arange(HB, dtype=jnp.int32)[None, :] < HB // 2
    owner = jnp.where(left_side, (owners_row - 1) % N_SUB, (owners_row + 1) % N_SUB)
    picked = jax.random.randint(jax.random.fold_in(key, 23), (N_SUB, HB), 0, GB_DEV)
    return (owner * GB_DEV + picked).astype(jnp.int32)


def touch_ends(entries, own_key, least, largest):
    longest = entries.shape.index(max(entries.shape))
    spots = []
    for shift in (0, 1):
        where = [jax.random.randint(jax.random.fold_in(own_key, axis), (), 0, length) for axis, length in enumerate(entries.shape)]
        where[longest] = (where[longest] + shift) % entries.shape[longest]
        spots.append(tuple(where))
    return entries.at[spots[0]].set(least).at[spots[1]].set(largest)


def shard_levels(stream_key, dims, cuts, low, largest):
    level = 1.0
    for position, blocks in cuts:
        draws = jax.random.uniform(jax.random.fold_in(jax.random.fold_in(stream_key, 6), position), (blocks,), jnp.float32, low / len(cuts), largest / len(cuts))
        level = level * jnp.repeat(jnp.exp(draws), dims[position] // blocks).reshape((-1,) + (1,) * (len(dims) - 1 - position))
    return level


def length_profile(number_of, total, reach, skew):
    weights = [(1 << 20) // math.isqrt(standing ** skew) + 1 for standing in range(2, number_of + 1)]
    surplus, given = total - reach - (number_of - 1), [1] * (number_of - 1)
    while surplus > 0:
        movable = [i for i in range(number_of - 1) if given[i] < reach]
        whole, left = sum([weights[i] for i in movable]), surplus
        for i in movable:
            extra = min(reach - given[i], max(1, left * weights[i] // whole), surplus)
            given[i] = given[i] + extra
            surplus = surplus - extra
    return np.array([reach] + given)


def uneven(rng, amount, total, bound, skew):
    if amount == 2:
        one = jax.random.randint(rng, (), max(1, total - bound), min(bound, total - 1) + 1)
        return jnp.stack([one, total - one])
    tallies = jnp.asarray(length_profile(amount, total, bound, skew), jnp.int32)
    twos = (amount - 1) // 2
    donor, sink = tallies[1:1 + 2 * twos:2], tallies[2:2 + 2 * twos:2]
    slack = jnp.minimum(donor - 1, bound - sink)
    shifted = jax.random.randint(jax.random.fold_in(rng, 1), (twos,), 0, 1 << 20) % (slack + 1)
    tallies = tallies.at[1:1 + 2 * twos:2].set(donor - shifted).at[2:2 + 2 * twos:2].set(sink + shifted)
    return tallies[jax.random.permutation(jax.random.fold_in(rng, 2), amount)]


def centred(key, extent, deviation, reach, cuts=(), held_as=jnp.bfloat16):
    entries = jax.random.normal(key, extent, jnp.float32) * deviation
    if len(cuts) > 0:
        entries = shard_levels(key, extent, cuts, -0.22, 0.18) * entries
    return jnp.clip(entries, min=-reach, max=reach).astype(held_as)


def setup_inputs(seed: int = 0) -> dict:
    key_of = jax.random.split(jax.random.key(seed), 9)
    return {
        "rhs": draw_rhs(jax.random.fold_in(key_of[8], 71), 0),
        "schur_diag": centred(key_of[1], (G, GB_DEV * BI), (GB_DEV * BI) ** -0.5, 0.375, ((0, 16),)),
        "precond": centred(key_of[2], (G, EXT), EXT ** -0.5, 0.25, ((0, 16),)),
        "halo_ids": draw_halo_ids(jax.random.fold_in(key_of[8], 71), 0),
        "factors": centred(key_of[4], (SLOTS, BLK, BLK), BLK ** -0.5, 0.1875, ((0, 128),)),
        "couplings": centred(key_of[5], (SLOTS, BLK, IFB * BI), (8 * IFB * BI) ** -0.5, 0.09375, ((0, 128),)),
        "block_ids": touch_ends(jax.random.randint(key_of[6], (SLOTS, IFB), 0, GBLK), jax.random.fold_in(key_of[6], 1), 0, GBLK - 1).astype(jnp.int32),
        "counts": uneven(key_of[7], DEVICES, DEVICES * NB_DEV * 5 // 8, NB_DEV, 2).astype(jnp.int32),
    }


def reference(rhs, schur_diag, precond, halo_ids, factors, couplings, block_ids, counts):
    group_rows = GB_DEV * BI
    highest = lax.Precision.HIGHEST

    def apply_schur(field):
        blocks = field.reshape(GBLK, BI, NRHS).astype(jnp.bfloat16)
        slot_index = jnp.arange(SLOTS, dtype=jnp.int32)
        live = slot_index % NB_DEV < counts[slot_index // NB_DEV]

        def step(total, item):
            factor, coupling, listed, flag = item

            def add_slot(carry):
                picked = blocks[listed].reshape(IFB * BI, NRHS)
                first = jnp.dot(coupling, picked, preferred_element_type=jnp.float32).astype(jnp.bfloat16)
                second = jnp.dot(factor, first, preferred_element_type=jnp.float32).astype(jnp.bfloat16)
                third = jnp.dot(factor.T, second, preferred_element_type=jnp.float32).astype(jnp.bfloat16)
                fourth = jnp.dot(coupling.T, third, preferred_element_type=jnp.float32)
                return carry.at[listed].add(fourth.reshape(IFB, BI, NRHS))
            return (lax.cond(flag, add_slot, lambda carry: carry, total), None)
        total, _ = lax.scan(step, jnp.zeros((GBLK, BI, NRHS), jnp.float32), (factors, couplings, block_ids, live))
        rounded = lax.optimization_barrier(field.astype(jnp.bfloat16)).astype(jnp.float32)
        local = jnp.einsum('dij,djr->dir', schur_diag.reshape(N_SUB, group_rows, group_rows).astype(jnp.float32), rounded.reshape(N_SUB, group_rows, NRHS), precision=highest)
        return 3.0 * field + local.reshape(G, NRHS) - total.reshape(G, NRHS)

    def precondition(field):
        groups = field.reshape(N_SUB, group_rows, NRHS)
        halo_rows = field.reshape(GBLK, BI, NRHS)[halo_ids].reshape(N_SUB, HB * BI, NRHS)
        extended = jnp.concatenate([groups, halo_rows], axis=1).astype(jnp.bfloat16)
        extended = lax.optimization_barrier(extended).astype(jnp.float32)
        product = jnp.einsum('dij,djr->dir', precond.reshape(N_SUB, group_rows, EXT).astype(jnp.float32), extended, precision=highest)
        return (groups + product).reshape(G, NRHS)

    def column_sums(left, right):
        return lax.optimization_barrier(jnp.sum(left * right, axis=0))
    start_norm = jnp.sqrt(column_sums(rhs, rhs))
    first_basis = rhs / start_norm
    first_dir = precondition(first_basis)
    first_image = apply_schur(first_dir)
    upper_one = column_sums(first_image, first_basis)
    rest_one = first_image - upper_one * first_basis
    length_one = jnp.sqrt(column_sums(rest_one, rest_one))
    second_basis = rest_one / length_one
    second_dir = precondition(second_basis)
    second_image = apply_schur(second_dir)
    upper_two = column_sums(second_image, first_basis)
    middle = column_sums(second_image, second_basis)
    rest_two = second_image - upper_two * first_basis - middle * second_basis
    length_two = jnp.sqrt(column_sums(rest_two, rest_two))
    radius_one = jnp.sqrt(upper_one * upper_one + length_one * length_one)
    cosine_one = upper_one / radius_one
    sine_one = length_one / radius_one
    rotated_top = cosine_one * upper_two + sine_one * middle
    rotated_low = cosine_one * middle - sine_one * upper_two
    weight_two = -rotated_low * sine_one * start_norm / (rotated_low * rotated_low + length_two * length_two)
    weight_one = (cosine_one * start_norm - rotated_top * weight_two) / radius_one
    return weight_one * first_dir + weight_two * second_dir
```

```python
import jax
import jax.numpy as jnp
from jax import lax
from jax.experimental import pallas as pl
from jax.experimental.pallas import tpu as pltpu
from jax.sharding import Mesh
from jax.sharding import PartitionSpec as P

BI = 128
ROWS = 256
COLS = 128
HALF = 64
PART = 16
GROUPS = 16
BLOCKS = 32
SUB = ("x", "y")
XYZ = ("x", "y", "z")
ALL = ("x", "y", "z", "c")
F32 = jnp.float32
BF16 = jnp.bfloat16
SHRINK = 2.0**-31
VMEM = pl.BlockSpec(memory_space=pltpu.VMEM)
SMEM = pl.BlockSpec(memory_space=pltpu.SMEM)
ANY = pl.BlockSpec(memory_space=pl.ANY)
NT = (((1,), (1,)), ((), ()))
NN = (((1,), (0,)), ((), ()))


def dot(left, right, dims=NN):
    return lax.dot_general(left, right, dims, preferred_element_type=F32)


def call(body, name, outs, specs, scratch=(), flops=0, moved=1 << 20):
    return pl.pallas_call(
        body,
        name=name,
        out_shape=outs,
        in_specs=specs,
        out_specs=[VMEM] * len(outs),
        scratch_shapes=list(scratch),
        cost_estimate=pl.CostEstimate(flops=flops, bytes_accessed=moved, transcendentals=0),
        compiler_params=pltpu.CompilerParams(vmem_limit_bytes=40 << 20),
    )


def out(shape, dtype):
    return jax.ShapeDtypeStruct(shape, dtype)


def opening(rhs, halo, sent):
    field = rhs[...]
    sums = jnp.sum(field * field, axis=0, keepdims=True)
    row = lax.broadcasted_iota(jnp.int32, (8, COLS), 0)
    left = (halo[0, 0] & 1).astype(F32)
    right = (halo[0, 1] & 1).astype(F32)
    tile = jnp.where(row == 0, sums, jnp.where(row == 1, left, jnp.where(row == 2, right, 0.0)))
    sent[...] = jnp.broadcast_to(tile[None], sent.shape)


def first_direction(
    pos, halo, rhs, before, after, facts, precond, diag, sent, z_nat, base, basis, turned
):
    beta = jnp.sqrt(jnp.sum(facts[:, 0:1, :], axis=0))
    v = rhs[...] / beta
    left = before[pl.ds(pl.multiple_of((halo[0, 0] & 1) * BI, BI), BI), :] / beta
    right = after[pl.ds(pl.multiple_of((halo[0, 1] & 1) * BI, BI), BI), :] / beta
    patch = jnp.concatenate([v, left, right], axis=0).astype(BF16)
    z = v + dot(precond[...], patch)
    z_nat[...] = z
    half = pl.ds(pl.multiple_of(pos[2] * HALF, HALF), HALF)
    part = pl.ds(pl.multiple_of(pos[2] * HALF + pos[1] * PART, PART), PART)
    turned[...] = z.T
    mine = turned[half, :].astype(BF16)
    sent[...] = jnp.broadcast_to(mine[None], sent.shape)
    turned[...] = (3.0 * z + dot(diag[...], z.astype(BF16))).T
    base[...] = turned[part, :]
    turned[...] = v.T
    basis[...] = turned[part, :]


def slots(
    ids, counts, near, far, couplings, factors, kept, given, coup, fact, picked, one, two, sems
):
    live = counts[0]

    def fetch(slot):
        return (
            pltpu.make_async_copy(couplings.at[slot], coup.at[slot], sems.at[slot, 0]),
            pltpu.make_async_copy(factors.at[slot], fact.at[slot], sems.at[slot, 1]),
        )

    for copy in fetch(0):
        copy.start()

    @pl.when(live > 1)
    def _():
        for copy in fetch(1):
            copy.start()

    @pl.when(live < 2)
    def _():
        kept[4:8] = jnp.zeros((4, HALF, BI), F32)
        given[4:8] = jnp.zeros((4, HALF, BI), F32)

    def step(slot, carry):
        for j in range(4):
            block = ids[slot, j]
            lanes = pl.ds(pl.multiple_of((block & 1) * BI, BI), BI)
            picked[0:HALF, j * BI : (j + 1) * BI] = near[block >> 1, :, lanes]
            picked[HALF:COLS, j * BI : (j + 1) * BI] = far[block >> 1, :, lanes]
        get_coup, get_fact = fetch(slot)
        get_coup.wait()
        for n in range(4):
            span = slice(n * 256, (n + 1) * 256)
            one[:, span] = dot(picked[...], coup[slot, span, :], NT).astype(BF16)
        get_fact.wait()
        for n in range(4):
            span = slice(n * 256, (n + 1) * 256)
            two[:, span] = dot(one[...], fact[slot, span, :], NT).astype(BF16)
        for n in range(4):
            span = slice(n * 256, (n + 1) * 256)
            one[:, span] = dot(two[...], fact[slot, :, span]).astype(BF16)
        for n in range(2):
            piece = dot(one[...], coup[slot, :, n * 256 : (n + 1) * 256])
            for m in range(2):
                lanes = slice(m * BI, (m + 1) * BI)
                kept[slot * 4 + n * 2 + m] = piece[0:HALF, lanes]
                given[slot * 4 + n * 2 + m] = piece[HALF:COLS, lanes]
        return carry

    lax.fori_loop(0, live, step, 0)


def parcels(ids, ids_far, kept, got, facts, sent, total):
    total[...] = jnp.zeros_like(total)
    for i in range(8):
        block = ids[i // 4, i % 4]
        total[block] = total[block] + kept[i]
    for i in range(8):
        block = ids_far[i // 4, i % 4]
        total[block] = total[block] + got[i]
    with_halo = sent.shape[2] > ROWS

    def group(d, carry):
        lower = 2 * ((d + GROUPS - 1) % GROUPS)
        upper = 2 * ((d + 1) % GROUPS)
        blocks = [total[2 * d], total[2 * d + 1]]
        if with_halo:
            left = facts[d, 1:2, :] > 0.5
            right = facts[d, 2:3, :] > 0.5
            blocks.append(jnp.where(left, total[lower + 1], total[lower]))
            blocks.append(jnp.where(right, total[upper + 1], total[upper]))
        for j, block in enumerate(blocks):
            low = block.astype(BF16)
            for z in range(4):
                sent[d * 4 + z, :, j * BI : (j + 1) * BI] = low[z * PART : (z + 1) * PART]
        return carry

    lax.fori_loop(0, GROUPS, group, 0)


def summed(arrived):
    def add(i, total):
        for j in range(8):
            total = total + arrived[i * 8 + j].astype(F32)
        return total

    return lax.fori_loop(0, 8, add, jnp.zeros(arrived.shape[1:], F32))


def second_direction(halo, arrived, base, before, after, precond, diag, sent, base_two, w):
    coupled = summed(arrived)
    left = before[:, pl.ds(pl.multiple_of((halo[0, 0] & 1) * BI, BI), BI)]
    right = after[:, pl.ds(pl.multiple_of((halo[0, 1] & 1) * BI, BI), BI)]
    image = base[...] - coupled[:, :ROWS]
    patch = jnp.concatenate(
        [
            image,
            left - coupled[:, ROWS : ROWS + BI],
            right - coupled[:, ROWS + BI :],
        ],
        axis=1,
    ).astype(BF16)
    z = image + dot(patch, precond[...], NT)
    low = z.astype(BF16)
    w[...] = image
    base_two[...] = 3.0 * z + dot(low, diag[...], NT)
    sent[...] = jnp.broadcast_to(low[None], sent.shape)


def products(pos, arrived, base, w, basis, sent):
    image = (base[...] - summed(arrived)) * SHRINK
    one = w[...]
    v = basis[...]
    lane = lax.broadcasted_iota(jnp.int32, (PART, COLS), 1)
    row = lax.broadcasted_iota(jnp.int32, (PART, COLS), 0)
    here = lane == row + (pos[2] * HALF + pos[1] * PART)
    rank = lax.broadcasted_iota(jnp.int32, (8, COLS), 0)
    tile = jnp.zeros((8, COLS), F32)
    pairs = [(v, one), (one, one), (v, image), (one, image), (image, image)]
    for k, (left, right) in enumerate(pairs):
        value = jnp.sum(left * right, axis=1, keepdims=True)
        spread = jnp.sum(jnp.where(here, value, 0.0), axis=0, keepdims=True)
        tile = jnp.where(rank == k, spread, tile)
    sent[...] = jnp.broadcast_to(tile[None], sent.shape)


def closing(pos, near, far, facts, z_one, z_near, z_far, answer):
    sums = jnp.sum(near[...], axis=0) + jnp.sum(far[...], axis=0)
    beta = jnp.sqrt(jnp.sum(facts[:, 0:1, :], axis=0))
    h11, ww, vx, wx, xx = (sums[k : k + 1] for k in range(5))
    h21 = jnp.sqrt(ww - h11 * h11)
    small = SHRINK * h11
    h12 = (vx - small * h11) / (SHRINK * h21)
    h22 = ((wx - h11 * vx) - small * ww + small * h11 * h11) / (SHRINK * h21) / h21
    scaled = SHRINK * h21
    norm = ((xx - 2.0 * small * wx) + small * small * ww) / scaled / scaled
    low_square = norm - h12 * h12 - h22 * h22
    rho = jnp.sqrt(h11 * h11 + h21 * h21)
    cosine = h11 / rho
    sine = h21 / rho
    top = cosine * h12 + sine * h22
    low = cosine * h22 - sine * h12
    y2 = -low * sine * beta / (low * low + low_square)
    y1 = (cosine * beta - top * y2) / rho
    second = y2 / h21
    first = y1 - second * h11
    a = z_near[0].astype(F32)
    b = z_far[0].astype(F32)
    swap = pos[2] == 1
    stacked = jnp.concatenate([jnp.where(swap, b, a), jnp.where(swap, a, b)], axis=0)
    answer[...] = first * z_one[...] + second * stacked.T


def other_core(array):
    return lax.ppermute(array, "c", [(0, 1), (1, 0)])


def swap_all(array, axes):
    return lax.all_to_all(array, axes, split_axis=0, concat_axis=0, tiled=True)


def neighbours(array):
    forward = lax.ppermute(array, SUB, [(i, (i + 1) % GROUPS) for i in range(GROUPS)])
    backward = lax.ppermute(array, SUB, [((i + 1) % GROUPS, i) for i in range(GROUPS)])
    return forward, backward


def on_device(rhs, schur_diag, precond, halo_ids, factors, couplings, block_ids, counts):
    group = lax.axis_index(SUB)
    pos = jnp.stack([group, lax.axis_index("z"), lax.axis_index("c")]).astype(jnp.int32)
    ids_far = other_core(block_ids)

    def apply_slots(near, far):
        return call(
            slots,
            "slots",
            [out((8, HALF, BI), F32), out((8, HALF, BI), F32)],
            [SMEM, SMEM, VMEM, VMEM, ANY, ANY],
            [
                pltpu.VMEM((2, 1024, 512), BF16),
                pltpu.VMEM((2, 1024, 1024), BF16),
                pltpu.VMEM((COLS, 512), BF16),
                pltpu.VMEM((COLS, 1024), BF16),
                pltpu.VMEM((COLS, 1024), BF16),
                pltpu.SemaphoreType.DMA((2, 2)),
            ],
            flops=2 * 805306368,
            moved=8 << 20,
        )(block_ids, counts, near, far, couplings, factors)

    def to_owners(kept, given, width):
        got = other_core(given)
        (sent,) = call(
            parcels,
            "parcels",
            [out((64, PART, width), BF16)],
            [SMEM, SMEM, VMEM, VMEM, VMEM],
            [pltpu.VMEM((BLOCKS, HALF, BI), F32)],
        )(block_ids, ids_far, kept, got, facts)
        return swap_all(sent, XYZ)

    before, after = neighbours(rhs)
    (opened,) = call(opening, "opening", [out((GROUPS, 8, COLS), F32)], [VMEM, SMEM])(
        rhs, halo_ids
    )
    facts = swap_all(opened, SUB)
    sent, z_one, base, basis = call(
        first_direction,
        "first_direction",
        [
            out((GROUPS, HALF, ROWS), BF16),
            out((ROWS, COLS), F32),
            out((PART, ROWS), F32),
            out((PART, ROWS), F32),
        ],
        [SMEM, SMEM, VMEM, VMEM, VMEM, VMEM, VMEM, VMEM],
        [pltpu.VMEM((COLS, ROWS), F32)],
        flops=1 << 26,
    )(pos, halo_ids, rhs, before, after, facts, precond, schur_diag)
    base_before, base_after = neighbours(base)
    near = swap_all(sent, SUB)
    far = other_core(near)
    kept, given = apply_slots(near, far)
    arrived = to_owners(kept, given, 2 * ROWS)
    sent, base, w = call(
        second_direction,
        "second_direction",
        [out((64, PART, ROWS), BF16), out((PART, ROWS), F32), out((PART, ROWS), F32)],
        [SMEM, VMEM, VMEM, VMEM, VMEM, VMEM, VMEM],
        flops=1 << 26,
    )(halo_ids, arrived, base, base_before, base_after, precond, schur_diag)
    near = swap_all(sent, XYZ).reshape(GROUPS, HALF, ROWS)
    far = other_core(near)
    kept, given = apply_slots(near, far)
    arrived = to_owners(kept, given, ROWS)
    (sent,) = call(
        products, "products", [out((64, 8, COLS), F32)], [SMEM, VMEM, VMEM, VMEM, VMEM]
    )(pos, arrived, base, w, basis)
    sums = swap_all(sent, XYZ)
    sums_far = other_core(sums)
    own = [lax.dynamic_slice_in_dim(half, group, 1, 0) for half in (near, far)]
    (answer,) = call(
        closing, "closing", [out((ROWS, COLS), F32)], [SMEM] + [VMEM] * 6
    )(pos, sums, sums_far, facts, z_one, *own)
    return answer


def solution(mesh):
    torus = Mesh(mesh.devices.reshape(4, 4, 4, 2), ALL)
    placed = (
        P(SUB, None),
        P(SUB, None),
        P(SUB, None),
        P(SUB, None),
        P(ALL, None, None),
        P(ALL, None, None),
        P(ALL, None),
        P(ALL),
    )
    return jax.shard_map(
        on_device, mesh=torus, in_specs=placed, out_specs=P(SUB, None), check_vma=False
    )
```

```python
import jax
import jax.numpy as jnp
from jax import lax
from jax.experimental import pallas as pl
from jax.experimental.pallas import tpu as pltpu
from jax.sharding import Mesh
from jax.sharding import PartitionSpec as P

BI = 128
ROWS = 256
COLS = 128
HALF = 64
PART = 16
GROUPS = 16
BLOCKS = 32
SUB = ("x", "y")
XYZ = ("x", "y", "z")
ALL = ("x", "y", "z", "c")
F32 = jnp.float32
BF16 = jnp.bfloat16
SHRINK = 2.0**-31
VMEM = pl.BlockSpec(memory_space=pltpu.VMEM)
SMEM = pl.BlockSpec(memory_space=pltpu.SMEM)
ANY = pl.BlockSpec(memory_space=pl.ANY)
HBM = pl.BlockSpec(memory_space=pltpu.HBM)
GROUP, DEPTH, CORE, LIVE, HALO, IDS = 0, 1, 2, 3, 4, 6
NT = (((1,), (1,)), ((), ()))
NN = (((1,), (0,)), ((), ()))


def dot(left, right, dims=NN):
    return lax.dot_general(left, right, dims, preferred_element_type=F32)


def call(body, outs, specs, scratch=(), flops=0, moved=1 << 20, room=4 << 20):
    return pl.pallas_call(
        body,
        out_shape=outs,
        in_specs=specs,
        out_specs=[VMEM] * len(outs),
        scratch_shapes=list(scratch),
        cost_estimate=pl.CostEstimate(flops=flops, bytes_accessed=moved, transcendentals=0),
        compiler_params=pltpu.CompilerParams(vmem_limit_bytes=room),
    )


def out(shape, dtype):
    return jax.ShapeDtypeStruct(shape, dtype)


def parity(table, place):
    return table[place] & 1


def block_at(table, place):
    return pl.ds(pl.multiple_of(parity(table, place) * BI, BI), BI)


def opening(table, rhs, sent, held):
    field = rhs[...]
    held[...] = field
    sums = jnp.sum(field * field, axis=0, keepdims=True)
    row = lax.broadcasted_iota(jnp.int32, (8, COLS), 0)
    left = parity(table, HALO).astype(F32)
    right = parity(table, HALO + 1).astype(F32)
    tile = jnp.where(row == 0, sums, jnp.where(row == 1, left, jnp.where(row == 2, right, 0.0)))
    sent[...] = jnp.broadcast_to(tile[None], sent.shape)


def bring_owned(precond, diag, precond_v, diag_v, sems):
    copies = [
        pltpu.make_async_copy(precond, precond_v, sems.at[0]),
        pltpu.make_async_copy(diag, diag_v, sems.at[1]),
    ]
    for copy in copies:
        copy.start()
    for copy in copies:
        copy.wait()


def bring_couplings(table, after, couplings, coup_v, sems):
    def copy(slot):
        return pltpu.make_async_copy(couplings.at[slot], coup_v.at[slot], sems.at[slot])

    copy(0).start()

    @pl.when(table[LIVE] > 1)
    def _():
        copy(1).start()
        copy(1).wait()

    copy(0).wait()


def first_direction(
    table, table_far, rhs, before, after, facts, precond, diag, sent, z_nat, base, basis, turned
):
    beta = jnp.sqrt(jnp.sum(facts[:, 0:1, :], axis=0))
    v = rhs[...] / beta
    left = before[block_at(table, HALO), :] / beta
    right = after[block_at(table, HALO + 1), :] / beta
    patch = jnp.concatenate([v, left, right], axis=0).astype(BF16)
    z = v + dot(precond[...], patch)
    z_nat[...] = z
    half = pl.ds(pl.multiple_of(table[CORE] * HALF, HALF), HALF)
    part = pl.ds(pl.multiple_of(table[CORE] * HALF + table[DEPTH] * PART, PART), PART)
    turned[...] = z.T
    mine = turned[half, :].astype(BF16)
    sent[...] = jnp.broadcast_to(mine[None], sent.shape)
    turned[...] = (3.0 * z + dot(diag[...], z.astype(BF16))).T
    base[...] = turned[part, :]
    turned[...] = v.T
    basis[...] = turned[part, :]


def slots(table, near, far, coup, factors, kept, given, fact, picked, one, two, sems):
    live = table[LIVE]

    def fetch(slot, n):
        span = pl.ds(n * 256, 256)
        return pltpu.make_async_copy(
            factors.at[slot, span], fact.at[slot, span], sems.at[slot, n]
        )

    for n in range(4):
        fetch(0, n).start()

    @pl.when(live > 1)
    def _():
        for n in range(4):
            fetch(1, n).start()

    @pl.when(live < 2)
    def _():
        kept[4:8] = jnp.zeros((4, HALF, BI), F32)
        given[4:8] = jnp.zeros((4, HALF, BI), F32)

    def step(slot, carry):
        for j in range(4):
            block = table[IDS + slot * 4 + j]
            lanes = pl.ds(pl.multiple_of((block & 1) * BI, BI), BI)
            picked[0:HALF, j * BI : (j + 1) * BI] = near[block >> 1, :, lanes]
            picked[HALF:COLS, j * BI : (j + 1) * BI] = far[block >> 1, :, lanes]
        for n in range(4):
            span = slice(n * 256, (n + 1) * 256)
            one[:, span] = dot(picked[...], coup[slot, span, :], NT).astype(BF16)
        for n in range(4):
            span = slice(n * 256, (n + 1) * 256)
            fetch(slot, n).wait()
            two[:, span] = dot(one[...], fact[slot, span, :], NT).astype(BF16)
        for n in range(4):
            span = slice(n * 256, (n + 1) * 256)
            one[:, span] = dot(two[...], fact[slot, :, span]).astype(BF16)
        for n in range(2):
            piece = dot(one[...], coup[slot, :, n * 256 : (n + 1) * 256])
            for m in range(2):
                lanes = slice(m * BI, (m + 1) * BI)
                kept[slot * 4 + n * 2 + m] = piece[0:HALF, lanes]
                given[slot * 4 + n * 2 + m] = piece[HALF:COLS, lanes]
        return carry

    lax.fori_loop(0, live, step, 0)


def parcels(table, table_far, kept, got, facts, base, sent, total):
    total[...] = jnp.zeros_like(total)
    for i in range(8):
        block = table[IDS + i]
        total[block] = total[block] + kept[i]
    for i in range(8):
        block = table_far[IDS + i]
        total[block] = total[block] + got[i]
    with_halo = sent.shape[2] > ROWS

    def group(d, carry):
        lower = 2 * ((d + GROUPS - 1) & (GROUPS - 1))
        upper = 2 * ((d + 1) & (GROUPS - 1))
        blocks = [total[2 * d], total[2 * d + 1]]
        if with_halo:
            left = facts[d, 1:2, :] > 0.5
            right = facts[d, 2:3, :] > 0.5
            blocks.append(jnp.where(left, total[lower + 1], total[lower]))
            blocks.append(jnp.where(right, total[upper + 1], total[upper]))
        for j, block in enumerate(blocks):
            low = block.astype(BF16)
            for z in range(4):
                sent[d * 4 + z, :, j * BI : (j + 1) * BI] = low[z * PART : (z + 1) * PART]
        return carry

    lax.fori_loop(0, GROUPS, group, 0)
    if with_halo:
        mine = table[GROUP]
        depth = table[DEPTH]
        part = pl.ds(pl.multiple_of(depth * PART, PART), PART)
        for side, other in ((0, mine + 1), (1, mine + GROUPS - 1)):
            other = other & (GROUPS - 1)
            upper = facts[other, side + 1 : side + 2, :] > 0.5
            block = jnp.where(upper, total[2 * mine + 1, part, :], total[2 * mine, part, :])
            stays = jnp.where(upper, base[:, BI:], base[:, :BI])
            lanes = slice(ROWS + side * BI, ROWS + (side + 1) * BI)
            sent[other * 4 + depth, :, lanes] = (block - stays).astype(BF16)


def summed(arrived):
    def add(i, total):
        for j in range(8):
            total = total + arrived[i * 8 + j].astype(F32)
        return total

    return lax.fori_loop(0, 8, add, jnp.zeros(arrived.shape[1:], F32))


def second_direction(arrived, base, precond, diag, sent, base_two, w):
    coupled = summed(arrived)
    image = base[...] - coupled[:, :ROWS]
    patch = jnp.concatenate([image, -coupled[:, ROWS:]], axis=1).astype(BF16)
    z = image + dot(patch, precond[...], NT)
    low = z.astype(BF16)
    w[...] = image
    base_two[...] = 3.0 * z + dot(low, diag[...], NT)
    sent[...] = jnp.broadcast_to(low[None], sent.shape)


def products(table, arrived, base, w, basis, sent):
    image = (base[...] - summed(arrived)) * SHRINK
    one = w[...]
    v = basis[...]
    lane = lax.broadcasted_iota(jnp.int32, (PART, COLS), 1)
    row = lax.broadcasted_iota(jnp.int32, (PART, COLS), 0)
    here = lane == row + (table[CORE] * HALF + table[DEPTH] * PART)
    rank = lax.broadcasted_iota(jnp.int32, (8, COLS), 0)
    tile = jnp.zeros((8, COLS), F32)
    pairs = [(v, one), (one, one), (v, image), (one, image), (image, image)]
    for k, (left, right) in enumerate(pairs):
        value = jnp.sum(left * right, axis=1, keepdims=True)
        spread = jnp.sum(jnp.where(here, value, 0.0), axis=0, keepdims=True)
        tile = jnp.where(rank == k, spread, tile)
    sent[...] = jnp.broadcast_to(tile[None], sent.shape)


def closing(table, near, far, facts, z_one, z_near, z_far, answer):
    sums = jnp.sum(near[...], axis=0) + jnp.sum(far[...], axis=0)
    beta = jnp.sqrt(jnp.sum(facts[:, 0:1, :], axis=0))
    h11, ww, vx, wx, xx = (sums[k : k + 1] for k in range(5))
    h21 = jnp.sqrt(ww - h11 * h11)
    small = SHRINK * h11
    h12 = (vx - small * h11) / (SHRINK * h21)
    h22 = ((wx - h11 * vx) - small * ww + small * h11 * h11) / (SHRINK * h21) / h21
    scaled = SHRINK * h21
    norm = ((xx - 2.0 * small * wx) + small * small * ww) / scaled / scaled
    low_square = norm - h12 * h12 - h22 * h22
    rho = jnp.sqrt(h11 * h11 + h21 * h21)
    cosine = h11 / rho
    sine = h21 / rho
    top = cosine * h12 + sine * h22
    low = cosine * h22 - sine * h12
    y2 = -low * sine * beta / (low * low + low_square)
    y1 = (cosine * beta - top * y2) / rho
    second = y2 / h21
    first = y1 - second * h11
    a = z_near[0].astype(F32)
    b = z_far[0].astype(F32)
    swap = table[CORE] == 1
    stacked = jnp.concatenate([jnp.where(swap, b, a), jnp.where(swap, a, b)], axis=0)
    answer[...] = first * z_one[...] + second * stacked.T


def other_core(array):
    return lax.ppermute(array, "c", [(0, 1), (1, 0)])


def swap_all(array, axes):
    return lax.all_to_all(array, axes, split_axis=0, concat_axis=0, tiled=True)


def neighbours(array):
    forward = lax.ppermute(array, SUB, [(i, (i + 1) % GROUPS) for i in range(GROUPS)])
    backward = lax.ppermute(array, SUB, [((i + 1) % GROUPS, i) for i in range(GROUPS)])
    return forward, backward


def on_device(rhs, schur_diag, precond, halo_ids, factors, couplings, block_ids, counts):
    group = lax.axis_index(SUB)
    place = jnp.stack([group, lax.axis_index("z"), lax.axis_index("c")]).astype(jnp.int32)
    table = jnp.concatenate([place, counts, halo_ids.reshape(-1), block_ids.reshape(-1)])
    table_far = other_core(table)

    def apply_slots(near, far):
        return call(
            slots,
            [out((8, HALF, BI), F32), out((8, HALF, BI), F32)],
            [SMEM, VMEM, VMEM, VMEM, HBM],
            [
                pltpu.VMEM((2, 1024, 1024), BF16),
                pltpu.VMEM((COLS, 512), BF16),
                pltpu.VMEM((COLS, 1024), BF16),
                pltpu.VMEM((COLS, 1024), BF16),
                pltpu.SemaphoreType.DMA((2, 4)),
            ],
            flops=2 * 805306368,
            moved=8 << 20,
            room=50000 << 10,
        )(table, near, far, coup_v, factors)

    def to_owners(kept, given, width):
        got = other_core(given)
        (sent,) = call(
            parcels,
            [out((64, PART, width), BF16)],
            [SMEM, SMEM, VMEM, VMEM, VMEM, VMEM],
            [pltpu.VMEM((BLOCKS, HALF, BI), F32)],
        )(table, table_far, kept, got, facts, base)
        return swap_all(sent, XYZ)

    opened, held = call(
        opening, [out((GROUPS, 8, COLS), F32), out((ROWS, COLS), F32)], [SMEM, VMEM]
    )(table, rhs)
    facts = swap_all(opened, SUB)
    before, after = neighbours(held)
    precond_v, diag_v = call(
        bring_owned,
        [out(a.shape, BF16) for a in (precond, schur_diag)],
        [HBM, HBM],
        [pltpu.SemaphoreType.DMA((2,))],
    )(precond, schur_diag)
    sent, z_one, base, basis = call(
        first_direction,
        [
            out((GROUPS, HALF, ROWS), BF16),
            out((ROWS, COLS), F32),
            out((PART, ROWS), F32),
            out((PART, ROWS), F32),
        ],
        [SMEM, SMEM, VMEM, VMEM, VMEM, VMEM, VMEM, VMEM],
        [pltpu.VMEM((COLS, ROWS), F32)],
        flops=1 << 26,
    )(table, table_far, held, before, after, facts, precond_v, diag_v)
    (coup_v,) = call(
        bring_couplings,
        [out(couplings.shape, BF16)],
        [SMEM, ANY, HBM],
        [pltpu.SemaphoreType.DMA((2,))],
        moved=12 << 20,
    )(table, base, couplings)
    near = swap_all(sent, SUB)
    far = other_core(near)
    kept, given = apply_slots(near, far)
    arrived = to_owners(kept, given, 2 * ROWS)
    sent, base, w = call(
        second_direction,
        [out((64, PART, ROWS), BF16), out((PART, ROWS), F32), out((PART, ROWS), F32)],
        [VMEM, VMEM, VMEM, VMEM],
        flops=1 << 26,
    )(arrived, base, precond_v, diag_v)
    near = swap_all(sent, XYZ).reshape(GROUPS, HALF, ROWS)
    far = other_core(near)
    kept, given = apply_slots(near, far)
    arrived = to_owners(kept, given, ROWS)
    (sent,) = call(
        products, [out((64, 8, COLS), F32)], [SMEM, VMEM, VMEM, VMEM, VMEM]
    )(table, arrived, base, w, basis)
    sums = swap_all(sent, XYZ)
    sums_far = other_core(sums)
    own = [lax.dynamic_slice_in_dim(half, group, 1, 0) for half in (near, far)]
    (answer,) = call(
        closing, [out((ROWS, COLS), F32)], [SMEM] + [VMEM] * 6
    )(table, sums, sums_far, facts, z_one, *own)
    return answer


def solution(mesh):
    torus = Mesh(mesh.devices.reshape(4, 4, 4, 2), ALL)
    placed = (
        P(SUB, None),
        P(SUB, None),
        P(SUB, None),
        P(SUB, None),
        P(ALL, None, None),
        P(ALL, None, None),
        P(ALL, None),
        P(ALL),
    )

    return jax.shard_map(
        on_device, mesh=torus, in_specs=placed, out_specs=P(SUB, None), check_vma=False
    )
```

```python
import jax
import jax.numpy as jnp
from jax import lax
from jax.experimental import pallas as pl
from jax.experimental.pallas import tpu as pltpu
from jax.sharding import Mesh
from jax.sharding import PartitionSpec as P

BI = 128
ROWS = 256
COLS = 128
HALF = 64
PART = 16
GROUPS = 16
BLOCKS = 32
SUB = ("x", "y")
XYZ = ("x", "y", "z")
ALL = ("x", "y", "z", "c")
F32 = jnp.float32
BF16 = jnp.bfloat16
SHRINK = 2.0**-31
VMEM = pl.BlockSpec(memory_space=pltpu.VMEM)
SMEM = pl.BlockSpec(memory_space=pltpu.SMEM)
ANY = pl.BlockSpec(memory_space=pl.ANY)
HBM = pl.BlockSpec(memory_space=pltpu.HBM)
GROUP, DEPTH, CORE, LIVE, HALO, IDS = 0, 1, 2, 3, 4, 6
NT = (((1,), (1,)), ((), ()))
NN = (((1,), (0,)), ((), ()))


def dot(left, right, dims=NN):
    return lax.dot_general(left, right, dims, preferred_element_type=F32)


def call(body, outs, specs, scratch=(), flops=0, moved=1 << 20, room=4 << 20):
    return pl.pallas_call(
        body,
        out_shape=outs,
        in_specs=specs,
        out_specs=[VMEM] * len(outs),
        scratch_shapes=list(scratch),
        cost_estimate=pl.CostEstimate(flops=flops, bytes_accessed=moved, transcendentals=0),
        compiler_params=pltpu.CompilerParams(vmem_limit_bytes=room),
    )


def out(shape, dtype):
    return jax.ShapeDtypeStruct(shape, dtype)


def parity(table, place):
    return table[place] & 1


def block_at(table, place):
    return pl.ds(pl.multiple_of(parity(table, place) * BI, BI), BI)


def opening(halo, rhs, sent, held, sems):
    copies = [
        pltpu.make_async_copy(rhs.at[pl.ds(i * 64, 64)], held.at[pl.ds(i * 64, 64)], sems.at[i])
        for i in range(4)
    ]
    for copy in copies:
        copy.start()
    sums = jnp.zeros((1, COLS), F32)
    for i, copy in enumerate(copies):
        copy.wait()
        field = held[i * 64 : (i + 1) * 64, :]
        sums = sums + jnp.sum(field * field, axis=0, keepdims=True)
    row = lax.broadcasted_iota(jnp.int32, (8, COLS), 0)
    left = (halo[0, 0] & 1).astype(F32)
    right = (halo[0, 1] & 1).astype(F32)
    tile = jnp.where(row == 0, sums, jnp.where(row == 1, left, jnp.where(row == 2, right, 0.0)))
    sent[...] = jnp.broadcast_to(tile[None], sent.shape)


def bring_owned(rhs, precond, diag, rhs_v, precond_v, diag_v, sems):
    copies = [
        pltpu.make_async_copy(rhs, rhs_v, sems.at[2]),
        pltpu.make_async_copy(precond, precond_v, sems.at[0]),
        pltpu.make_async_copy(diag, diag_v, sems.at[1]),
    ]
    for copy in copies:
        copy.start()
    for copy in copies:
        copy.wait()


def bring_coupling(after, couplings, coup, sem):
    copy = pltpu.make_async_copy(couplings.at[0], coup, sem)
    copy.start()
    copy.wait()


def first_direction(
    table, table_far, rhs, paired, linked, facts, precond, diag, sent, z_nat, base, basis, turned
):
    beta = jnp.sqrt(jnp.sum(facts[:, 0:1, :], axis=0))
    v = rhs[...] / beta
    odd = (table[GROUP] & 1) == 1
    lower = block_at(table, HALO)
    upper = block_at(table, HALO + 1)
    left = jnp.where(odd, paired[lower, :], linked[lower, :]) / beta
    right = jnp.where(odd, linked[upper, :], paired[upper, :]) / beta
    patch = jnp.concatenate([v, left, right], axis=0).astype(BF16)
    z = v + dot(precond[...], patch)
    z_nat[...] = z
    half = pl.ds(pl.multiple_of(table[CORE] * HALF, HALF), HALF)
    part = pl.ds(pl.multiple_of(table[CORE] * HALF + table[DEPTH] * PART, PART), PART)
    turned[...] = z.T
    mine = turned[half, :].astype(BF16)
    sent[...] = jnp.broadcast_to(mine[None], sent.shape)
    turned[...] = (3.0 * z + dot(diag[...], z.astype(BF16))).T
    base[...] = turned[part, :]
    turned[...] = v.T
    basis[...] = turned[part, :]


def slots(
    table,
    near,
    far,
    coup_a,
    couplings,
    factors,
    kept,
    given,
    coup_b,
    fact_a,
    fact_b,
    picked,
    one,
    two,
    sems,
):
    spans = [pl.ds(n * 256, 256) for n in range(4)]
    first = [
        pltpu.make_async_copy(factors.at[0, span], fact_a.at[span], sems.at[n])
        for n, span in enumerate(spans)
    ]
    second = [pltpu.make_async_copy(couplings.at[1], coup_b, sems.at[4])] + [
        pltpu.make_async_copy(factors.at[1, span], fact_b.at[span], sems.at[5 + n])
        for n, span in enumerate(spans)
    ]
    for copy in first:
        copy.start()

    @pl.when(table[LIVE] > 1)
    def _():
        for copy in second:
            copy.start()

    def slot(number, coup, fact, copies):
        for j in range(4):
            block = table[IDS + number * 4 + j]
            lanes = pl.ds(pl.multiple_of((block & 1) * BI, BI), BI)
            picked[0:HALF, j * BI : (j + 1) * BI] = near[block >> 1, :, lanes]
            picked[HALF:COLS, j * BI : (j + 1) * BI] = far[block >> 1, :, lanes]
        for n in range(4):
            span = slice(n * 256, (n + 1) * 256)
            one[:, span] = dot(picked[...], coup[span, :], NT).astype(BF16)
        for n in range(4):
            span = slice(n * 256, (n + 1) * 256)
            copies[n].wait()
            two[:, span] = dot(one[...], fact[span, :], NT).astype(BF16)
        for n in range(4):
            span = slice(n * 256, (n + 1) * 256)
            one[:, span] = dot(two[...], fact[:, span]).astype(BF16)
        for n in range(2):
            piece = dot(one[...], coup[:, n * 256 : (n + 1) * 256])
            for m in range(2):
                lanes = slice(m * BI, (m + 1) * BI)
                kept[number * 4 + n * 2 + m] = piece[0:HALF, lanes]
                given[number * 4 + n * 2 + m] = piece[HALF:COLS, lanes]

    slot(0, coup_a, fact_a, first)

    @pl.when(table[LIVE] > 1)
    def _():
        second[0].wait()
        slot(1, coup_b, fact_b, second[1:])

    @pl.when(table[LIVE] < 2)
    def _():
        kept[4:8] = jnp.zeros((4, HALF, BI), F32)
        given[4:8] = jnp.zeros((4, HALF, BI), F32)


def parcels(table, table_far, kept, got, facts, base, sent, total):
    total[...] = jnp.zeros_like(total)
    for i in range(8):
        block = table[IDS + i]
        total[block] = total[block] + kept[i]
    for i in range(8):
        block = table_far[IDS + i]
        total[block] = total[block] + got[i]
    with_halo = sent.shape[2] > ROWS

    def group(d, carry):
        lower = 2 * ((d + GROUPS - 1) & (GROUPS - 1))
        upper = 2 * ((d + 1) & (GROUPS - 1))
        blocks = [total[2 * d], total[2 * d + 1]]
        if with_halo:
            left = facts[d, 1:2, :] > 0.5
            right = facts[d, 2:3, :] > 0.5
            blocks.append(jnp.where(left, total[lower + 1], total[lower]))
            blocks.append(jnp.where(right, total[upper + 1], total[upper]))
        for j, block in enumerate(blocks):
            low = block.astype(BF16)
            for z in range(4):
                sent[d * 4 + z, :, j * BI : (j + 1) * BI] = low[z * PART : (z + 1) * PART]
        return carry

    lax.fori_loop(0, GROUPS, group, 0)
    if with_halo:
        mine = table[GROUP]
        depth = table[DEPTH]
        part = pl.ds(pl.multiple_of(depth * PART, PART), PART)
        for side, other in ((0, mine + 1), (1, mine + GROUPS - 1)):
            other = other & (GROUPS - 1)
            upper = facts[other, side + 1 : side + 2, :] > 0.5
            block = jnp.where(upper, total[2 * mine + 1, part, :], total[2 * mine, part, :])
            stays = jnp.where(upper, base[:, BI:], base[:, :BI])
            lanes = slice(ROWS + side * BI, ROWS + (side + 1) * BI)
            sent[other * 4 + depth, :, lanes] = (block - stays).astype(BF16)


def summed(arrived):
    def add(i, total):
        for j in range(8):
            total = total + arrived[i * 8 + j].astype(F32)
        return total

    return lax.fori_loop(0, 8, add, jnp.zeros(arrived.shape[1:], F32))


def second_direction(arrived, base, precond, diag, sent, base_two, w):
    coupled = summed(arrived)
    image = base[...] - coupled[:, :ROWS]
    patch = jnp.concatenate([image, -coupled[:, ROWS:]], axis=1).astype(BF16)
    z = image + dot(patch, precond[...], NT)
    low = z.astype(BF16)
    w[...] = image
    base_two[...] = 3.0 * z + dot(low, diag[...], NT)
    sent[...] = jnp.broadcast_to(low[None], sent.shape)


def products(table, arrived, base, w, basis, sent):
    image = (base[...] - summed(arrived)) * SHRINK
    one = w[...]
    v = basis[...]
    lane = lax.broadcasted_iota(jnp.int32, (PART, COLS), 1)
    row = lax.broadcasted_iota(jnp.int32, (PART, COLS), 0)
    here = lane == row + (table[CORE] * HALF + table[DEPTH] * PART)
    rank = lax.broadcasted_iota(jnp.int32, (8, COLS), 0)
    tile = jnp.zeros((8, COLS), F32)
    pairs = [(v, one), (one, one), (v, image), (one, image), (image, image)]
    for k, (left, right) in enumerate(pairs):
        value = jnp.sum(left * right, axis=1, keepdims=True)
        spread = jnp.sum(jnp.where(here, value, 0.0), axis=0, keepdims=True)
        tile = jnp.where(rank == k, spread, tile)
    sent[...] = jnp.broadcast_to(tile[None], sent.shape)


def closing(table, near, far, facts, z_one, z_near, z_far, answer):
    sums = jnp.sum(near[...], axis=0) + jnp.sum(far[...], axis=0)
    beta = jnp.sqrt(jnp.sum(facts[:, 0:1, :], axis=0))
    h11, ww, vx, wx, xx = (sums[k : k + 1] for k in range(5))
    h21 = jnp.sqrt(ww - h11 * h11)
    small = SHRINK * h11
    h12 = (vx - small * h11) / (SHRINK * h21)
    h22 = ((wx - h11 * vx) - small * ww + small * h11 * h11) / (SHRINK * h21) / h21
    scaled = SHRINK * h21
    norm = ((xx - 2.0 * small * wx) + small * small * ww) / scaled / scaled
    low_square = norm - h12 * h12 - h22 * h22
    rho = jnp.sqrt(h11 * h11 + h21 * h21)
    cosine = h11 / rho
    sine = h21 / rho
    top = cosine * h12 + sine * h22
    low = cosine * h22 - sine * h12
    y2 = -low * sine * beta / (low * low + low_square)
    y1 = (cosine * beta - top * y2) / rho
    second = y2 / h21
    first = y1 - second * h11
    a = z_near[0].astype(F32)
    b = z_far[0].astype(F32)
    swap = table[CORE] == 1
    stacked = jnp.concatenate([jnp.where(swap, b, a), jnp.where(swap, a, b)], axis=0)
    answer[...] = first * z_one[...] + second * stacked.T


def other_core(array):
    return lax.ppermute(array, "c", [(0, 1), (1, 0)])


def swap_all(array, axes):
    return lax.all_to_all(array, axes, split_axis=0, concat_axis=0, tiled=True)


def neighbours(array):
    paired = lax.ppermute(array, SUB, [(i, i ^ 1) for i in range(GROUPS)])
    linked = lax.ppermute(array, SUB, [(i, (i - 1 + 2 * (i & 1)) % GROUPS) for i in range(GROUPS)])
    return paired, linked


def on_device(rhs, schur_diag, precond, halo_ids, factors, couplings, block_ids, counts):
    group = lax.axis_index(SUB)
    place = jnp.stack([group, lax.axis_index("z"), lax.axis_index("c")]).astype(jnp.int32)
    table = jnp.concatenate([place, counts, halo_ids.reshape(-1), block_ids.reshape(-1)])
    table_far = other_core(table)

    def apply_slots(near, far):
        return call(
            slots,
            [out((8, HALF, BI), F32), out((8, HALF, BI), F32)],
            [SMEM] + [VMEM] * 3 + [HBM] * 2,
            [
                pltpu.VMEM((1024, 512), BF16),
                pltpu.VMEM((1024, 1024), BF16),
                pltpu.VMEM((1024, 1024), BF16),
                pltpu.VMEM((COLS, 512), BF16),
                pltpu.VMEM((COLS, 1024), BF16),
                pltpu.VMEM((COLS, 1024), BF16),
                pltpu.SemaphoreType.DMA((9,)),
            ],
            flops=2 * 805306368,
            moved=8 << 20,
            room=51000 << 10,
        )(table, near, far, coupling, couplings, factors)

    def to_owners(kept, given, width):
        got = other_core(given)
        (sent,) = call(
            parcels,
            [out((64, PART, width), BF16)],
            [SMEM, SMEM, VMEM, VMEM, VMEM, VMEM],
            [pltpu.VMEM((BLOCKS, HALF, BI), F32)],
        )(table, table_far, kept, got, facts, base)
        return swap_all(sent, XYZ)

    paired, linked = neighbours(rhs)
    (opened,) = call(
        opening,
        [out((GROUPS, 8, COLS), F32)],
        [SMEM, HBM],
        [pltpu.VMEM((ROWS, COLS), F32), pltpu.SemaphoreType.DMA((4,))],
        room=67043328,
    )(halo_ids, rhs)
    facts = swap_all(opened, SUB)
    rhs_v, precond_v, diag_v = call(
        bring_owned,
        [out(rhs.shape, F32), out(precond.shape, BF16), out(schur_diag.shape, BF16)],
        [HBM, HBM, HBM],
        [pltpu.SemaphoreType.DMA((3,))],
    )(rhs, precond, schur_diag)
    sent, z_one, base, basis = call(
        first_direction,
        [
            out((GROUPS, HALF, ROWS), BF16),
            out((ROWS, COLS), F32),
            out((PART, ROWS), F32),
            out((PART, ROWS), F32),
        ],
        [SMEM, SMEM, VMEM, VMEM, VMEM, VMEM, VMEM, VMEM],
        [pltpu.VMEM((COLS, ROWS), F32)],
        flops=1 << 26,
    )(table, table_far, rhs_v, paired, linked, facts, precond_v, diag_v)
    (coupling,) = call(
        bring_coupling,
        [out((1024, 512), BF16)],
        [ANY, HBM],
        [pltpu.SemaphoreType.DMA],
        moved=12 << 20,
    )(base, couplings)
    near = swap_all(sent, SUB)
    far = other_core(near)
    kept, given = apply_slots(near, far)
    arrived = to_owners(kept, given, 2 * ROWS)
    sent, base, w = call(
        second_direction,
        [out((64, PART, ROWS), BF16), out((PART, ROWS), F32), out((PART, ROWS), F32)],
        [VMEM, VMEM, VMEM, VMEM],
        flops=1 << 26,
    )(arrived, base, precond_v, diag_v)
    near = swap_all(sent, XYZ).reshape(GROUPS, HALF, ROWS)
    far = other_core(near)
    kept, given = apply_slots(near, far)
    arrived = to_owners(kept, given, ROWS)
    (sent,) = call(
        products, [out((64, 8, COLS), F32)], [SMEM, VMEM, VMEM, VMEM, VMEM]
    )(table, arrived, base, w, basis)
    sums = swap_all(sent, XYZ)
    sums_far = other_core(sums)
    own = [lax.dynamic_slice_in_dim(half, group, 1, 0) for half in (near, far)]
    (answer,) = call(
        closing, [out((ROWS, COLS), F32)], [SMEM] + [VMEM] * 6
    )(table, sums, sums_far, facts, z_one, *own)
    return answer


def solution(mesh):
    torus = Mesh(mesh.devices.reshape(4, 4, 4, 2), ALL)
    placed = (
        P(SUB, None),
        P(SUB, None),
        P(SUB, None),
        P(SUB, None),
        P(ALL, None, None),
        P(ALL, None, None),
        P(ALL, None),
        P(ALL),
    )

    return jax.shard_map(
        on_device, mesh=torus, in_specs=placed, out_specs=P(SUB, None), check_vma=False
    )
```

```python
import jax
import jax.numpy as jnp
from jax import lax
from jax.experimental import pallas as pl
from jax.experimental.pallas import tpu as pltpu
from jax.sharding import Mesh
from jax.sharding import PartitionSpec as P

BI = 128
ROWS = 256
COLS = 128
HALF = 64
PART = 16
GROUPS = 16
BLOCKS = 32
SUB = ("x", "y")
YX = ("y", "x")
YXZ = ("y", "x", "z")
ALL = ("x", "y", "z", "c")
F32 = jnp.float32
BF16 = jnp.bfloat16
SHRINK = 2.0**-31
VMEM = pl.BlockSpec(memory_space=pltpu.VMEM)
SMEM = pl.BlockSpec(memory_space=pltpu.SMEM)
ANY = pl.BlockSpec(memory_space=pl.ANY)
HBM = pl.BlockSpec(memory_space=pltpu.HBM)
GROUP, DEPTH, CORE, LIVE, HALO, IDS = 0, 1, 2, 3, 4, 6
NT = (((1,), (1,)), ((), ()))
NN = (((1,), (0,)), ((), ()))


def dot(left, right, dims=NN):
    return lax.dot_general(left, right, dims, preferred_element_type=F32)


def call(body, name, outs, specs, scratch=(), flops=0, moved=1 << 20, room=4 << 20):
    return pl.pallas_call(
        body,
        name=name,
        out_shape=outs,
        in_specs=specs,
        out_specs=[VMEM] * len(outs),
        scratch_shapes=list(scratch),
        cost_estimate=pl.CostEstimate(flops=flops, bytes_accessed=moved, transcendentals=0),
        compiler_params=pltpu.CompilerParams(vmem_limit_bytes=room),
    )


def out(shape, dtype):
    return jax.ShapeDtypeStruct(shape, dtype)


def partner(group):
    return ((group & 3) << 2) | (group >> 2)


def block_at(table, place):
    return pl.ds(pl.multiple_of((table[place] & 1) * BI, BI), BI)


def opening(halo, rhs, sent, held):
    field = rhs[...]
    held[...] = field
    sums = jnp.sum(field * field, axis=0, keepdims=True)
    row = lax.broadcasted_iota(jnp.int32, (8, COLS), 0)
    left = (halo[0, 0] & 1).astype(F32)
    right = (halo[0, 1] & 1).astype(F32)
    tile = jnp.where(row == 0, sums, jnp.where(row == 1, left, jnp.where(row == 2, right, 0.0)))
    sent[...] = jnp.broadcast_to(tile[None], sent.shape)


def bring_owned(precond, diag, precond_v, diag_v, sems):
    copies = [
        pltpu.make_async_copy(precond, precond_v, sems.at[0]),
        pltpu.make_async_copy(diag, diag_v, sems.at[1]),
    ]
    for copy in copies:
        copy.start()
    for copy in copies:
        copy.wait()


def bring_coupling(couplings, coup, sem):
    copy = pltpu.make_async_copy(couplings.at[0], coup, sem)
    copy.start()
    copy.wait()


def first_direction(
    table, table_far, rhs, paired, linked, facts, precond, diag, sent, z_nat, base, basis, turned
):
    beta = jnp.sqrt(jnp.sum(facts[:, 0:1, :], axis=0))
    v = rhs[...] / beta
    odd = (table[GROUP] & 1) == 1
    lower = block_at(table, HALO)
    upper = block_at(table, HALO + 1)
    left = jnp.where(odd, paired[lower, :], linked[lower, :]) / beta
    right = jnp.where(odd, linked[upper, :], paired[upper, :]) / beta
    patch = jnp.concatenate([v, left, right], axis=0).astype(BF16)
    z = v + dot(precond[...], patch)
    z_nat[...] = z
    half = pl.ds(pl.multiple_of(table[CORE] * HALF, HALF), HALF)
    part = pl.ds(pl.multiple_of(table[CORE] * HALF + table[DEPTH] * PART, PART), PART)
    turned[...] = z.T
    mine = turned[half, :].astype(BF16)
    sent[...] = jnp.broadcast_to(mine[None], sent.shape)
    turned[...] = (3.0 * z + dot(diag[...], z.astype(BF16))).T
    base[...] = turned[part, :]
    turned[...] = v.T
    basis[...] = turned[part, :]


def slots(
    table,
    near,
    far,
    coup_a,
    couplings,
    factors,
    kept,
    given,
    coup_b,
    fact_a,
    fact_b,
    picked,
    one,
    two,
    sems,
):
    first = pltpu.make_async_copy(factors.at[0], fact_a, sems.at[0])
    second = [
        pltpu.make_async_copy(couplings.at[1], coup_b, sems.at[1]),
        pltpu.make_async_copy(factors.at[1], fact_b, sems.at[2]),
    ]
    first.start()

    @pl.when(table[LIVE] > 1)
    def _():
        for copy in second:
            copy.start()

    def slot(number, coup, fact, copy):
        for j in range(4):
            block = table[IDS + number * 4 + j]
            place = partner(block >> 1)
            lanes = pl.ds(pl.multiple_of((block & 1) * BI, BI), BI)
            picked[0:HALF, j * BI : (j + 1) * BI] = near[place, :, lanes]
            picked[HALF:COLS, j * BI : (j + 1) * BI] = far[place, :, lanes]
        for n in range(4):
            span = slice(n * 256, (n + 1) * 256)
            one[:, span] = dot(picked[...], coup[span, :], NT).astype(BF16)
        copy.wait()
        for n in range(4):
            span = slice(n * 256, (n + 1) * 256)
            two[:, span] = dot(one[...], fact[span, :], NT).astype(BF16)
        for n in range(4):
            span = slice(n * 256, (n + 1) * 256)
            one[:, span] = dot(two[...], fact[:, span]).astype(BF16)
        for n in range(2):
            piece = dot(one[...], coup[:, n * 256 : (n + 1) * 256])
            for m in range(2):
                lanes = slice(m * BI, (m + 1) * BI)
                kept[number * 4 + n * 2 + m] = piece[0:HALF, lanes]
                given[number * 4 + n * 2 + m] = piece[HALF:COLS, lanes]

    slot(0, coup_a, fact_a, first)

    @pl.when(table[LIVE] > 1)
    def _():
        second[0].wait()
        slot(1, coup_b, fact_b, second[1])

    @pl.when(table[LIVE] < 2)
    def _():
        kept[4:8] = jnp.zeros((4, HALF, BI), F32)
        given[4:8] = jnp.zeros((4, HALF, BI), F32)


def parcels(table, table_far, kept, got, facts, base, sent, total):
    total[...] = jnp.zeros_like(total)
    for i in range(8):
        block = table[IDS + i]
        total[block] = total[block] + kept[i]
    for i in range(8):
        block = table_far[IDS + i]
        total[block] = total[block] + got[i]
    with_halo = sent.shape[2] > ROWS

    def group(d, carry):
        place = partner(d)
        lower = 2 * ((d + GROUPS - 1) & (GROUPS - 1))
        upper = 2 * ((d + 1) & (GROUPS - 1))
        blocks = [total[2 * d], total[2 * d + 1]]
        if with_halo:
            left = facts[place, 1:2, :] > 0.5
            right = facts[place, 2:3, :] > 0.5
            blocks.append(jnp.where(left, total[lower + 1], total[lower]))
            blocks.append(jnp.where(right, total[upper + 1], total[upper]))
        for j, block in enumerate(blocks):
            low = block.astype(BF16)
            for z in range(4):
                sent[place * 4 + z, :, j * BI : (j + 1) * BI] = low[z * PART : (z + 1) * PART]
        return carry

    lax.fori_loop(0, GROUPS, group, 0)
    if with_halo:
        mine = table[GROUP]
        depth = table[DEPTH]
        part = pl.ds(pl.multiple_of(depth * PART, PART), PART)
        for side, other in ((0, mine + 1), (1, mine + GROUPS - 1)):
            other = partner(other & (GROUPS - 1))
            upper = facts[other, side + 1 : side + 2, :] > 0.5
            block = jnp.where(upper, total[2 * mine + 1, part, :], total[2 * mine, part, :])
            stays = jnp.where(upper, base[:, BI:], base[:, :BI])
            lanes = slice(ROWS + side * BI, ROWS + (side + 1) * BI)
            sent[other * 4 + depth, :, lanes] = (block - stays).astype(BF16)


def summed(arrived):
    def add(i, total):
        for j in range(8):
            total = total + arrived[i * 8 + j].astype(F32)
        return total

    return lax.fori_loop(0, 8, add, jnp.zeros(arrived.shape[1:], F32))


def second_direction(arrived, base, precond, diag, sent, base_two, w):
    coupled = summed(arrived)
    image = base[...] - coupled[:, :ROWS]
    patch = jnp.concatenate([image, -coupled[:, ROWS:]], axis=1).astype(BF16)
    z = image + dot(patch, precond[...], NT)
    low = z.astype(BF16)
    w[...] = image
    base_two[...] = 3.0 * z + dot(low, diag[...], NT)
    sent[...] = jnp.broadcast_to(low[None], sent.shape)


def products(table, arrived, base, w, basis, sent):
    image = (base[...] - summed(arrived)) * SHRINK
    one = w[...]
    v = basis[...]
    lane = lax.broadcasted_iota(jnp.int32, (PART, COLS), 1)
    row = lax.broadcasted_iota(jnp.int32, (PART, COLS), 0)
    here = lane == row + (table[CORE] * HALF + table[DEPTH] * PART)
    rank = lax.broadcasted_iota(jnp.int32, (8, COLS), 0)
    tile = jnp.zeros((8, COLS), F32)
    pairs = [(v, one), (one, one), (v, image), (one, image), (image, image)]
    for k, (left, right) in enumerate(pairs):
        value = jnp.sum(left * right, axis=1, keepdims=True)
        spread = jnp.sum(jnp.where(here, value, 0.0), axis=0, keepdims=True)
        tile = jnp.where(rank == k, spread, tile)
    sent[...] = jnp.broadcast_to(tile[None], sent.shape)


def closing(table, near, far, facts, z_one, z_near, z_far, answer):
    sums = jnp.sum(near[...], axis=0) + jnp.sum(far[...], axis=0)
    beta = jnp.sqrt(jnp.sum(facts[:, 0:1, :], axis=0))
    h11, ww, vx, wx, xx = (sums[k : k + 1] for k in range(5))
    h21 = jnp.sqrt(ww - h11 * h11)
    small = SHRINK * h11
    h12 = (vx - small * h11) / (SHRINK * h21)
    h22 = ((wx - h11 * vx) - small * ww + small * h11 * h11) / (SHRINK * h21) / h21
    scaled = SHRINK * h21
    norm = ((xx - 2.0 * small * wx) + small * small * ww) / scaled / scaled
    low_square = norm - h12 * h12 - h22 * h22
    rho = jnp.sqrt(h11 * h11 + h21 * h21)
    cosine = h11 / rho
    sine = h21 / rho
    top = cosine * h12 + sine * h22
    low = cosine * h22 - sine * h12
    y2 = -low * sine * beta / (low * low + low_square)
    y1 = (cosine * beta - top * y2) / rho
    second = y2 / h21
    first = y1 - second * h11
    a = z_near[0].astype(F32)
    b = z_far[0].astype(F32)
    swap = table[CORE] == 1
    stacked = jnp.concatenate([jnp.where(swap, b, a), jnp.where(swap, a, b)], axis=0)
    answer[...] = first * z_one[...] + second * stacked.T


def other_core(array):
    return lax.ppermute(array, "c", [(0, 1), (1, 0)])


def swap_all(array, axes):
    return lax.all_to_all(array, axes, split_axis=0, concat_axis=0, tiled=True)


def neighbours(array):
    paired = lax.ppermute(array, SUB, [(i, i ^ 1) for i in range(GROUPS)])
    linked = lax.ppermute(array, SUB, [(i, (i - 1 + 2 * (i & 1)) % GROUPS) for i in range(GROUPS)])
    return paired, linked


def on_device(rhs, schur_diag, precond, halo_ids, factors, couplings, block_ids, counts):
    group = lax.axis_index(SUB)
    place = jnp.stack([group, lax.axis_index("z"), lax.axis_index("c")]).astype(jnp.int32)
    table = jnp.concatenate([place, counts, halo_ids.reshape(-1), block_ids.reshape(-1)])
    table_far = other_core(table)

    def apply_slots(near, far):
        return call(
            slots,
            "slots",
            [out((8, HALF, BI), F32), out((8, HALF, BI), F32)],
            [SMEM] + [VMEM] * 3 + [HBM] * 2,
            [
                pltpu.VMEM((1024, 512), BF16),
                pltpu.VMEM((1024, 1024), BF16),
                pltpu.VMEM((1024, 1024), BF16),
                pltpu.VMEM((COLS, 512), BF16),
                pltpu.VMEM((COLS, 1024), BF16),
                pltpu.VMEM((COLS, 1024), BF16),
                pltpu.SemaphoreType.DMA((3,)),
            ],
            flops=2 * 805306368,
            moved=8 << 20,
            room=51000 << 10,
        )(table, near, far, coupling, couplings, factors)

    def to_owners(kept, given, width):
        got = other_core(given)
        (sent,) = call(
            parcels,
            "parcels",
            [out((64, PART, width), BF16)],
            [SMEM, SMEM, VMEM, VMEM, VMEM, VMEM],
            [pltpu.VMEM((BLOCKS, HALF, BI), F32)],
        )(table, table_far, kept, got, facts, base)
        return swap_all(sent, YXZ)

    paired, linked = neighbours(rhs)
    opened, held = call(
        opening,
        "opening",
        [out((GROUPS, 8, COLS), F32), out((ROWS, COLS), F32)],
        [SMEM, VMEM],
    )(halo_ids, rhs)
    facts = swap_all(opened, YX)
    precond_v, diag_v = call(
        bring_owned,
        "bring_owned",
        [out(precond.shape, BF16), out(schur_diag.shape, BF16)],
        [HBM, HBM],
        [pltpu.SemaphoreType.DMA((2,))],
    )(precond, schur_diag)
    (coupling,) = call(
        bring_coupling,
        "bring_coupling",
        [out((1024, 512), BF16)],
        [HBM],
        [pltpu.SemaphoreType.DMA],
    )(couplings)
    sent, z_one, base, basis = call(
        first_direction,
        "first_direction",
        [
            out((GROUPS, HALF, ROWS), BF16),
            out((ROWS, COLS), F32),
            out((PART, ROWS), F32),
            out((PART, ROWS), F32),
        ],
        [SMEM, SMEM, VMEM, VMEM, VMEM, VMEM, VMEM, VMEM],
        [pltpu.VMEM((COLS, ROWS), F32)],
        flops=1 << 26,
    )(table, table_far, held, paired, linked, facts, precond_v, diag_v)
    near = swap_all(sent, YX)
    far = other_core(near)
    kept, given = apply_slots(near, far)
    arrived = to_owners(kept, given, 2 * ROWS)
    sent, base, w = call(
        second_direction,
        "second_direction",
        [out((64, PART, ROWS), BF16), out((PART, ROWS), F32), out((PART, ROWS), F32)],
        [VMEM, VMEM, VMEM, VMEM],
        flops=1 << 26,
    )(arrived, base, precond_v, diag_v)
    near = swap_all(sent, YXZ).reshape(GROUPS, HALF, ROWS)
    far = other_core(near)
    kept, given = apply_slots(near, far)
    arrived = to_owners(kept, given, ROWS)
    (sent,) = call(
        products, "products", [out((64, 8, COLS), F32)], [SMEM, VMEM, VMEM, VMEM, VMEM]
    )(table, arrived, base, w, basis)
    sums = swap_all(sent, YXZ)
    sums_far = other_core(sums)
    own = [lax.dynamic_slice_in_dim(half, partner(group), 1, 0) for half in (near, far)]
    (answer,) = call(
        closing, "closing", [out((ROWS, COLS), F32)], [SMEM] + [VMEM] * 6
    )(table, sums, sums_far, facts, z_one, *own)
    return answer


def solution(mesh):
    torus = Mesh(mesh.devices.reshape(4, 4, 4, 2), ALL)
    placed = (
        P(SUB, None),
        P(SUB, None),
        P(SUB, None),
        P(SUB, None),
        P(ALL, None, None),
        P(ALL, None, None),
        P(ALL, None),
        P(ALL),
    )
    return jax.shard_map(
        on_device, mesh=torus, in_specs=placed, out_specs=P(SUB, None), check_vma=False
    )
```

```python
import jax
import jax.numpy as jnp
from jax import lax
from jax.experimental import pallas as pl
from jax.experimental.pallas import tpu as pltpu
from jax.sharding import Mesh
from jax.sharding import PartitionSpec as P

BI = 128
ROWS = 256
COLS = 128
HALF = 64
PART = 16
GROUPS = 16
BLOCKS = 32
SUB = ("x", "y")
YX = ("y", "x")
YXZ = ("y", "x", "z")
ALL = ("x", "y", "z", "c")
F32 = jnp.float32
BF16 = jnp.bfloat16
SHRINK = 2.0**-31
VMEM = pl.BlockSpec(memory_space=pltpu.VMEM)
SMEM = pl.BlockSpec(memory_space=pltpu.SMEM)
ANY = pl.BlockSpec(memory_space=pl.ANY)
HBM = pl.BlockSpec(memory_space=pltpu.HBM)
GROUP, DEPTH, CORE, LIVE, HALO, IDS = 0, 1, 2, 3, 4, 6
NT = (((1,), (1,)), ((), ()))
NN = (((1,), (0,)), ((), ()))


def dot(left, right, dims=NN):
    return lax.dot_general(left, right, dims, preferred_element_type=F32)


def call(body, name, outs, specs, scratch=(), flops=0, moved=1 << 20, room=4 << 20):
    return pl.pallas_call(
        body,
        name=name,
        out_shape=outs,
        in_specs=specs,
        out_specs=[VMEM] * len(outs),
        scratch_shapes=list(scratch),
        cost_estimate=pl.CostEstimate(flops=flops, bytes_accessed=moved, transcendentals=0),
        compiler_params=pltpu.CompilerParams(vmem_limit_bytes=room),
    )


def out(shape, dtype):
    return jax.ShapeDtypeStruct(shape, dtype)


def partner(group):
    return ((group & 3) << 2) | (group >> 2)


def block_at(table, place):
    return pl.ds(pl.multiple_of((table[place] & 1) * BI, BI), BI)


def opening(place, halo, rhs, sent, turned):
    turned[...] = rhs[...].T
    part = pl.ds(pl.multiple_of(place[CORE] * HALF + place[DEPTH] * PART, PART), PART)
    row = lax.broadcasted_iota(jnp.int32, (8, ROWS), 0)
    left = (halo[0, 0] & 1).astype(F32)
    right = (halo[0, 1] & 1).astype(F32)
    tile = jnp.where(row == 0, left, jnp.where(row == 1, right, 0.0))
    mine = jnp.concatenate([turned[part, :], tile], axis=0)
    sent[...] = jnp.broadcast_to(mine[None], sent.shape)


def bring_owned(precond, diag, precond_v, diag_v, sems):
    copies = [
        pltpu.make_async_copy(precond, precond_v, sems.at[0]),
        pltpu.make_async_copy(diag, diag_v, sems.at[1]),
    ]
    for copy in copies:
        copy.start()
    for copy in copies:
        copy.wait()


def bring_coupling(couplings, coup, sem):
    copy = pltpu.make_async_copy(couplings.at[0], coup, sem)
    copy.start()
    copy.wait()


def first_direction(table, table_far, facts, precond, diag, sent, base, basis, scale):
    squares = jnp.zeros((PART, ROWS), F32)
    for i in range(GROUPS):
        squares = squares + facts[i, :PART, :] * facts[i, :PART, :]
    beta = jnp.sqrt(jnp.sum(squares, axis=1, keepdims=True))
    scale[...] = jnp.broadcast_to(beta, scale.shape)
    mine = table[GROUP]
    before = partner((mine + GROUPS - 1) & (GROUPS - 1))
    after = partner((mine + 1) & (GROUPS - 1))
    v = facts[partner(mine), :PART, :] / beta
    left = facts[before, :PART, block_at(table, HALO)] / beta
    right = facts[after, :PART, block_at(table, HALO + 1)] / beta
    basis[...] = v
    patch = jnp.concatenate([v, left, right], axis=1).astype(BF16)
    z = v + dot(patch, precond[...], NT)
    low = z.astype(BF16)
    base[...] = 3.0 * z + dot(low, diag[...], NT)
    sent[...] = jnp.broadcast_to(low[None], sent.shape)


def slots(
    table,
    near,
    far,
    coup_a,
    couplings,
    factors,
    kept,
    given,
    coup_b,
    fact_a,
    fact_b,
    picked,
    one,
    two,
    sems,
):
    first = pltpu.make_async_copy(factors.at[0], fact_a, sems.at[0])
    second = [
        pltpu.make_async_copy(couplings.at[1], coup_b, sems.at[1]),
        pltpu.make_async_copy(factors.at[1], fact_b, sems.at[2]),
    ]
    first.start()

    @pl.when(table[LIVE] > 1)
    def _():
        for copy in second:
            copy.start()

    def slot(number, coup, fact, copy):
        for j in range(4):
            block = table[IDS + number * 4 + j]
            place = partner(block >> 1)
            lanes = pl.ds(pl.multiple_of((block & 1) * BI, BI), BI)
            picked[0:HALF, j * BI : (j + 1) * BI] = near[place, :, lanes]
            picked[HALF:COLS, j * BI : (j + 1) * BI] = far[place, :, lanes]
        for n in range(4):
            span = slice(n * 256, (n + 1) * 256)
            one[:, span] = dot(picked[...], coup[span, :], NT).astype(BF16)
        copy.wait()
        for n in range(4):
            span = slice(n * 256, (n + 1) * 256)
            two[:, span] = dot(one[...], fact[span, :], NT).astype(BF16)
        for n in range(4):
            span = slice(n * 256, (n + 1) * 256)
            one[:, span] = dot(two[...], fact[:, span]).astype(BF16)
        for n in range(2):
            piece = dot(one[...], coup[:, n * 256 : (n + 1) * 256])
            for m in range(2):
                lanes = slice(m * BI, (m + 1) * BI)
                kept[number * 4 + n * 2 + m] = piece[0:HALF, lanes]
                given[number * 4 + n * 2 + m] = piece[HALF:COLS, lanes]

    slot(0, coup_a, fact_a, first)

    @pl.when(table[LIVE] > 1)
    def _():
        second[0].wait()
        slot(1, coup_b, fact_b, second[1])

    @pl.when(table[LIVE] < 2)
    def _():
        kept[4:8] = jnp.zeros((4, HALF, BI), F32)
        given[4:8] = jnp.zeros((4, HALF, BI), F32)


def parcels(table, table_far, kept, got, facts, base, sent, total):
    total[...] = jnp.zeros_like(total)
    for i in range(8):
        block = table[IDS + i]
        total[block] = total[block] + kept[i]
    for i in range(8):
        block = table_far[IDS + i]
        total[block] = total[block] + got[i]
    with_halo = sent.shape[2] > ROWS

    def group(d, carry):
        place = partner(d)
        lower = 2 * ((d + GROUPS - 1) & (GROUPS - 1))
        upper = 2 * ((d + 1) & (GROUPS - 1))
        blocks = [total[2 * d], total[2 * d + 1]]
        if with_halo:
            left = facts[place, PART : PART + 1, :BI] > 0.5
            right = facts[place, PART + 1 : PART + 2, :BI] > 0.5
            blocks.append(jnp.where(left, total[lower + 1], total[lower]))
            blocks.append(jnp.where(right, total[upper + 1], total[upper]))
        for j, block in enumerate(blocks):
            low = block.astype(BF16)
            for z in range(4):
                sent[place * 4 + z, :, j * BI : (j + 1) * BI] = low[z * PART : (z + 1) * PART]
        return carry

    lax.fori_loop(0, GROUPS, group, 0)
    if with_halo:
        mine = table[GROUP]
        depth = table[DEPTH]
        part = pl.ds(pl.multiple_of(depth * PART, PART), PART)
        for side, other in ((0, mine + 1), (1, mine + GROUPS - 1)):
            other = partner(other & (GROUPS - 1))
            upper = facts[other, PART + side : PART + side + 1, :BI] > 0.5
            block = jnp.where(upper, total[2 * mine + 1, part, :], total[2 * mine, part, :])
            stays = jnp.where(upper, base[:, BI:], base[:, :BI])
            lanes = slice(ROWS + side * BI, ROWS + (side + 1) * BI)
            sent[other * 4 + depth, :, lanes] = (block - stays).astype(BF16)


def summed(arrived):
    def add(i, total):
        for j in range(8):
            total = total + arrived[i * 8 + j].astype(F32)
        return total

    return lax.fori_loop(0, 8, add, jnp.zeros(arrived.shape[1:], F32))


def second_direction(arrived, base, precond, diag, sent, base_two, w):
    coupled = summed(arrived)
    image = base[...] - coupled[:, :ROWS]
    patch = jnp.concatenate([image, -coupled[:, ROWS:]], axis=1).astype(BF16)
    z = image + dot(patch, precond[...], NT)
    low = z.astype(BF16)
    w[...] = image
    base_two[...] = 3.0 * z + dot(low, diag[...], NT)
    sent[...] = jnp.broadcast_to(low[None], sent.shape)


def products(table, arrived, base, w, basis, scale, sent):
    image = (base[...] - summed(arrived)) * SHRINK
    one = w[...]
    v = basis[...]
    lane = lax.broadcasted_iota(jnp.int32, (PART, COLS), 1)
    row = lax.broadcasted_iota(jnp.int32, (PART, COLS), 0)
    here = lane == row + (table[CORE] * HALF + table[DEPTH] * PART)
    rank = lax.broadcasted_iota(jnp.int32, (8, COLS), 0)
    tile = jnp.zeros((8, COLS), F32)
    pairs = [(v, one), (one, one), (v, image), (one, image), (image, image)]
    for k, (left, right) in enumerate(pairs):
        value = jnp.sum(left * right, axis=1, keepdims=True)
        spread = jnp.sum(jnp.where(here, value, 0.0), axis=0, keepdims=True)
        tile = jnp.where(rank == k, spread, tile)
    beta = jnp.sum(jnp.where(here, scale[...] / GROUPS, 0.0), axis=0, keepdims=True)
    tile = jnp.where(rank == len(pairs), beta, tile)
    sent[...] = jnp.broadcast_to(tile[None], sent.shape)


def closing(table, near, far, one_near, one_far, two_near, two_far, answer):
    sums = jnp.sum(near[...], axis=0) + jnp.sum(far[...], axis=0)
    h11, ww, vx, wx, xx, beta = (sums[k : k + 1] for k in range(6))
    h21 = jnp.sqrt(ww - h11 * h11)
    small = SHRINK * h11
    h12 = (vx - small * h11) / (SHRINK * h21)
    h22 = ((wx - h11 * vx) - small * ww + small * h11 * h11) / (SHRINK * h21) / h21
    scaled = SHRINK * h21
    norm = ((xx - 2.0 * small * wx) + small * small * ww) / scaled / scaled
    low_square = norm - h12 * h12 - h22 * h22
    rho = jnp.sqrt(h11 * h11 + h21 * h21)
    cosine = h11 / rho
    sine = h21 / rho
    top = cosine * h12 + sine * h22
    low = cosine * h22 - sine * h12
    y2 = -low * sine * beta / (low * low + low_square)
    y1 = (cosine * beta - top * y2) / rho
    second = y2 / h21
    first = y1 - second * h11
    swap = table[CORE] == 1
    field = []
    for weight, own, other in ((first, one_near, one_far), (second, two_near, two_far)):
        a = own[0].astype(F32)
        b = other[0].astype(F32)
        stacked = jnp.concatenate([jnp.where(swap, b, a), jnp.where(swap, a, b)], axis=0)
        field.append(weight * stacked.T)
    answer[...] = field[0] + field[1]


def other_core(array):
    return lax.ppermute(array, "c", [(0, 1), (1, 0)])


def swap_all(array, axes):
    return lax.all_to_all(array, axes, split_axis=0, concat_axis=0, tiled=True)


def on_device(rhs, schur_diag, precond, halo_ids, factors, couplings, block_ids, counts):
    group = lax.axis_index(SUB)
    place = jnp.stack([group, lax.axis_index("z"), lax.axis_index("c")]).astype(jnp.int32)
    table = jnp.concatenate([place, counts, halo_ids.reshape(-1), block_ids.reshape(-1)])
    table_far = other_core(table)

    def gather(sent):
        near = swap_all(sent, YXZ).reshape(GROUPS, HALF, ROWS)
        far = other_core(near)
        mine = [lax.dynamic_slice_in_dim(half, partner(group), 1, 0) for half in (near, far)]
        return near, far, mine

    def apply_slots(near, far):
        return call(
            slots,
            "slots",
            [out((8, HALF, BI), F32), out((8, HALF, BI), F32)],
            [SMEM] + [VMEM] * 3 + [HBM] * 2,
            [
                pltpu.VMEM((1024, 512), BF16),
                pltpu.VMEM((1024, 1024), BF16),
                pltpu.VMEM((1024, 1024), BF16),
                pltpu.VMEM((COLS, 512), BF16),
                pltpu.VMEM((COLS, 1024), BF16),
                pltpu.VMEM((COLS, 1024), BF16),
                pltpu.SemaphoreType.DMA((3,)),
            ],
            flops=2 * 805306368,
            moved=8 << 20,
            room=51000 << 10,
        )(table, near, far, coupling, couplings, factors)

    def to_owners(kept, given, width):
        got = other_core(given)
        (sent,) = call(
            parcels,
            "parcels",
            [out((64, PART, width), BF16)],
            [SMEM, SMEM, VMEM, VMEM, VMEM, VMEM],
            [pltpu.VMEM((BLOCKS, HALF, BI), F32)],
        )(table, table_far, kept, got, facts, base)
        return swap_all(sent, YXZ)

    (opened,) = call(
        opening,
        "opening",
        [out((GROUPS, PART + 8, ROWS), F32)],
        [SMEM, SMEM, VMEM],
        [pltpu.VMEM((COLS, ROWS), F32)],
        room=67043328,
    )(place, halo_ids, rhs)
    facts = swap_all(opened, YX)
    precond_v, diag_v = call(
        bring_owned,
        "bring_owned",
        [out(precond.shape, BF16), out(schur_diag.shape, BF16)],
        [HBM, HBM],
        [pltpu.SemaphoreType.DMA((2,))],
    )(precond, schur_diag)
    (coupling,) = call(
        bring_coupling,
        "bring_coupling",
        [out((1024, 512), BF16)],
        [HBM],
        [pltpu.SemaphoreType.DMA],
    )(couplings)
    sent, base, basis, scale = call(
        first_direction,
        "first_direction",
        [
            out((64, PART, ROWS), BF16),
            out((PART, ROWS), F32),
            out((PART, ROWS), F32),
            out((PART, COLS), F32),
        ],
        [SMEM, SMEM, VMEM, VMEM, VMEM],
        flops=1 << 26,
    )(table, table_far, facts, precond_v, diag_v)
    near, far, mine = gather(sent)
    kept, given = apply_slots(near, far)
    arrived = to_owners(kept, given, 2 * ROWS)
    sent, base, w = call(
        second_direction,
        "second_direction",
        [out((64, PART, ROWS), BF16), out((PART, ROWS), F32), out((PART, ROWS), F32)],
        [VMEM, VMEM, VMEM, VMEM],
        flops=1 << 26,
    )(arrived, base, precond_v, diag_v)
    near, far, mine_two = gather(sent)
    kept, given = apply_slots(near, far)
    arrived = to_owners(kept, given, ROWS)
    (sent,) = call(
        products, "products", [out((64, 8, COLS), F32)], [SMEM] + [VMEM] * 5
    )(table, arrived, base, w, basis, scale)
    sums = swap_all(sent, YXZ)
    sums_far = other_core(sums)
    (answer,) = call(
        closing, "closing", [out((ROWS, COLS), F32)], [SMEM] + [VMEM] * 6
    )(table, sums, sums_far, *mine, *mine_two)
    return answer


def solution(mesh):
    torus = Mesh(mesh.devices.reshape(4, 4, 4, 2), ALL)
    placed = (
        P(SUB, None),
        P(SUB, None),
        P(SUB, None),
        P(SUB, None),
        P(ALL, None, None),
        P(ALL, None, None),
        P(ALL, None),
        P(ALL),
    )
    return jax.shard_map(
        on_device, mesh=torus, in_specs=placed, out_specs=P(SUB, None), check_vma=False
    )
```

```python
import jax
import jax.numpy as jnp
from jax import lax
from jax.experimental import pallas as pl
from jax.experimental.pallas import tpu as pltpu
from jax.sharding import Mesh
from jax.sharding import PartitionSpec as P

BI = 128
ROWS = 256
COLS = 128
HALF = 64
PART = 16
GROUPS = 16
BLOCKS = 32
SUB = ("x", "y")
YX = ("y", "x")
YXZ = ("y", "x", "z")
ALL = ("x", "y", "z", "c")
F32 = jnp.float32
BF16 = jnp.bfloat16
SHRINK = 2.0**-31
VMEM = pl.BlockSpec(memory_space=pltpu.VMEM)
SMEM = pl.BlockSpec(memory_space=pltpu.SMEM)
ANY = pl.BlockSpec(memory_space=pl.ANY)
HBM = pl.BlockSpec(memory_space=pltpu.HBM)
GROUP, DEPTH, CORE, LIVE, HALO, IDS = 0, 1, 2, 3, 4, 6
NT = (((1,), (1,)), ((), ()))
NN = (((1,), (0,)), ((), ()))


def dot(left, right, dims=NN):
    return lax.dot_general(left, right, dims, preferred_element_type=F32)


def call(body, name, outs, specs, scratch=(), flops=0, moved=1 << 20, room=4 << 20):
    return pl.pallas_call(
        body,
        name=name,
        out_shape=outs,
        in_specs=specs,
        out_specs=[VMEM] * len(outs),
        scratch_shapes=list(scratch),
        cost_estimate=pl.CostEstimate(flops=flops, bytes_accessed=moved, transcendentals=0),
        compiler_params=pltpu.CompilerParams(vmem_limit_bytes=room),
    )


def out(shape, dtype):
    return jax.ShapeDtypeStruct(shape, dtype)


def partner(group):
    return ((group & 3) << 2) | (group >> 2)


def block_at(table, place):
    return pl.ds(pl.multiple_of((table[place] & 1) * BI, BI), BI)


def opening(halo, rhs, sent, held):
    field = rhs[...]
    held[...] = field
    sums = jnp.sum(field * field, axis=0, keepdims=True)
    row = lax.broadcasted_iota(jnp.int32, (8, COLS), 0)
    left = (halo[0, 0] & 1).astype(F32)
    right = (halo[0, 1] & 1).astype(F32)
    tile = jnp.where(row == 0, sums, jnp.where(row == 1, left, jnp.where(row == 2, right, 0.0)))
    sent[...] = jnp.broadcast_to(tile[None], sent.shape)


def bring_owned(precond, diag, precond_v, diag_v, sems):
    copies = [
        pltpu.make_async_copy(precond, precond_v, sems.at[0]),
        pltpu.make_async_copy(diag, diag_v, sems.at[1]),
    ]
    for copy in copies:
        copy.start()
    for copy in copies:
        copy.wait()


def bring_slot(couplings, factors, coup, fact, sems):
    copies = [
        pltpu.make_async_copy(couplings.at[0], coup, sems.at[0]),
        pltpu.make_async_copy(factors.at[0], fact, sems.at[1]),
    ]
    for copy in copies:
        copy.start()
    for copy in copies:
        copy.wait()


def first_direction(
    table, table_far, rhs, paired, linked, facts, precond, diag, sent, z_nat, base, basis, turned
):
    beta = jnp.sqrt(jnp.sum(facts[:, 0:1, :], axis=0))
    v = rhs[...] / beta
    odd = (table[GROUP] & 1) == 1
    lower = block_at(table, HALO)
    upper = block_at(table, HALO + 1)
    left = jnp.where(odd, paired[lower, :], linked[lower, :]) / beta
    right = jnp.where(odd, linked[upper, :], paired[upper, :]) / beta
    patch = jnp.concatenate([v, left, right], axis=0).astype(BF16)
    z = v + dot(precond[...], patch)
    z_nat[...] = z
    half = pl.ds(pl.multiple_of(table[CORE] * HALF, HALF), HALF)
    part = pl.ds(pl.multiple_of(table[CORE] * HALF + table[DEPTH] * PART, PART), PART)
    turned[...] = z.T
    mine = turned[half, :].astype(BF16)
    sent[...] = jnp.broadcast_to(mine[None], sent.shape)
    turned[...] = (3.0 * z + dot(diag[...], z.astype(BF16))).T
    base[...] = turned[part, :]
    turned[...] = v.T
    basis[...] = turned[part, :]


def slots(
    table,
    near,
    far,
    coup_a,
    fact_a,
    couplings,
    factors,
    kept,
    given,
    coup_b,
    fact_b,
    picked,
    one,
    two,
    sems,
):
    second = [
        pltpu.make_async_copy(couplings.at[1], coup_b, sems.at[0]),
        pltpu.make_async_copy(factors.at[1], fact_b, sems.at[1]),
    ]

    @pl.when(table[LIVE] > 1)
    def _():
        for copy in second:
            copy.start()

    def slot(number, coup, fact):
        for j in range(4):
            block = table[IDS + number * 4 + j]
            place = partner(block >> 1)
            lanes = pl.ds(pl.multiple_of((block & 1) * BI, BI), BI)
            picked[0:HALF, j * BI : (j + 1) * BI] = near[place, :, lanes]
            picked[HALF:COLS, j * BI : (j + 1) * BI] = far[place, :, lanes]
        for n in range(4):
            span = slice(n * 256, (n + 1) * 256)
            one[:, span] = dot(picked[...], coup[span, :], NT).astype(BF16)
        for n in range(4):
            span = slice(n * 256, (n + 1) * 256)
            two[:, span] = dot(one[...], fact[span, :], NT).astype(BF16)
        for n in range(4):
            span = slice(n * 256, (n + 1) * 256)
            one[:, span] = dot(two[...], fact[:, span]).astype(BF16)
        for n in range(2):
            piece = dot(one[...], coup[:, n * 256 : (n + 1) * 256])
            for m in range(2):
                lanes = slice(m * BI, (m + 1) * BI)
                kept[number * 4 + n * 2 + m] = piece[0:HALF, lanes]
                given[number * 4 + n * 2 + m] = piece[HALF:COLS, lanes]

    slot(0, coup_a, fact_a)

    @pl.when(table[LIVE] > 1)
    def _():
        for copy in second:
            copy.wait()
        slot(1, coup_b, fact_b)

    @pl.when(table[LIVE] < 2)
    def _():
        kept[4:8] = jnp.zeros((4, HALF, BI), F32)
        given[4:8] = jnp.zeros((4, HALF, BI), F32)


def parcels(table, table_far, kept, got, facts, base, sent, total):
    total[...] = jnp.zeros_like(total)
    for i in range(8):
        block = table[IDS + i]
        total[block] = total[block] + kept[i]
    for i in range(8):
        block = table_far[IDS + i]
        total[block] = total[block] + got[i]
    with_halo = sent.shape[2] > ROWS

    def group(d, carry):
        place = partner(d)
        lower = 2 * ((d + GROUPS - 1) & (GROUPS - 1))
        upper = 2 * ((d + 1) & (GROUPS - 1))
        blocks = [total[2 * d], total[2 * d + 1]]
        if with_halo:
            left = facts[place, 1:2, :] > 0.5
            right = facts[place, 2:3, :] > 0.5
            blocks.append(jnp.where(left, total[lower + 1], total[lower]))
            blocks.append(jnp.where(right, total[upper + 1], total[upper]))
        for j, block in enumerate(blocks):
            low = block.astype(BF16)
            for z in range(4):
                sent[place * 4 + z, :, j * BI : (j + 1) * BI] = low[z * PART : (z + 1) * PART]
        return carry

    lax.fori_loop(0, GROUPS, group, 0)
    if with_halo:
        mine = table[GROUP]
        depth = table[DEPTH]
        part = pl.ds(pl.multiple_of(depth * PART, PART), PART)
        for side, other in ((0, mine + 1), (1, mine + GROUPS - 1)):
            other = partner(other & (GROUPS - 1))
            upper = facts[other, side + 1 : side + 2, :] > 0.5
            block = jnp.where(upper, total[2 * mine + 1, part, :], total[2 * mine, part, :])
            stays = jnp.where(upper, base[:, BI:], base[:, :BI])
            lanes = slice(ROWS + side * BI, ROWS + (side + 1) * BI)
            sent[other * 4 + depth, :, lanes] = (block - stays).astype(BF16)


def summed(arrived):
    def add(i, total):
        for j in range(8):
            total = total + arrived[i * 8 + j].astype(F32)
        return total

    return lax.fori_loop(0, 8, add, jnp.zeros(arrived.shape[1:], F32))


def second_direction(arrived, base, precond, diag, sent, base_two, w):
    coupled = summed(arrived)
    image = base[...] - coupled[:, :ROWS]
    patch = jnp.concatenate([image, -coupled[:, ROWS:]], axis=1).astype(BF16)
    z = image + dot(patch, precond[...], NT)
    low = z.astype(BF16)
    w[...] = image
    base_two[...] = 3.0 * z + dot(low, diag[...], NT)
    sent[...] = jnp.broadcast_to(low[None], sent.shape)


def products(table, arrived, base, w, basis, sent):
    image = (base[...] - summed(arrived)) * SHRINK
    one = w[...]
    v = basis[...]
    lane = lax.broadcasted_iota(jnp.int32, (PART, COLS), 1)
    row = lax.broadcasted_iota(jnp.int32, (PART, COLS), 0)
    here = lane == row + (table[CORE] * HALF + table[DEPTH] * PART)
    rank = lax.broadcasted_iota(jnp.int32, (8, COLS), 0)
    tile = jnp.zeros((8, COLS), F32)
    pairs = [(v, one), (one, one), (v, image), (one, image), (image, image)]
    for k, (left, right) in enumerate(pairs):
        value = jnp.sum(left * right, axis=1, keepdims=True)
        spread = jnp.sum(jnp.where(here, value, 0.0), axis=0, keepdims=True)
        tile = jnp.where(rank == k, spread, tile)
    sent[...] = jnp.broadcast_to(tile[None], sent.shape)


def closing(table, near, far, facts, z_one, z_near, z_far, answer):
    sums = jnp.sum(near[...], axis=0) + jnp.sum(far[...], axis=0)
    beta = jnp.sqrt(jnp.sum(facts[:, 0:1, :], axis=0))
    h11, ww, vx, wx, xx = (sums[k : k + 1] for k in range(5))
    h21 = jnp.sqrt(ww - h11 * h11)
    small = SHRINK * h11
    h12 = (vx - small * h11) / (SHRINK * h21)
    h22 = ((wx - h11 * vx) - small * ww + small * h11 * h11) / (SHRINK * h21) / h21
    scaled = SHRINK * h21
    norm = ((xx - 2.0 * small * wx) + small * small * ww) / scaled / scaled
    low_square = norm - h12 * h12 - h22 * h22
    rho = jnp.sqrt(h11 * h11 + h21 * h21)
    cosine = h11 / rho
    sine = h21 / rho
    top = cosine * h12 + sine * h22
    low = cosine * h22 - sine * h12
    y2 = -low * sine * beta / (low * low + low_square)
    y1 = (cosine * beta - top * y2) / rho
    second = y2 / h21
    first = y1 - second * h11
    a = z_near[0].astype(F32)
    b = z_far[0].astype(F32)
    swap = table[CORE] == 1
    stacked = jnp.concatenate([jnp.where(swap, b, a), jnp.where(swap, a, b)], axis=0)
    answer[...] = first * z_one[...] + second * stacked.T


def other_core(array):
    return lax.ppermute(array, "c", [(0, 1), (1, 0)])


def swap_all(array, axes):
    return lax.all_to_all(array, axes, split_axis=0, concat_axis=0, tiled=True)


def neighbours(array):
    paired = lax.ppermute(array, SUB, [(i, i ^ 1) for i in range(GROUPS)])
    linked = lax.ppermute(array, SUB, [(i, (i - 1 + 2 * (i & 1)) % GROUPS) for i in range(GROUPS)])
    return paired, linked


def on_device(rhs, schur_diag, precond, halo_ids, factors, couplings, block_ids, counts):
    group = lax.axis_index(SUB)
    place = jnp.stack([group, lax.axis_index("z"), lax.axis_index("c")]).astype(jnp.int32)
    table = jnp.concatenate([place, counts, halo_ids.reshape(-1), block_ids.reshape(-1)])
    table_far = other_core(table)

    def apply_slots(near, far):
        return call(
            slots,
            "slots",
            [out((8, HALF, BI), F32), out((8, HALF, BI), F32)],
            [SMEM] + [VMEM] * 4 + [HBM] * 2,
            [
                pltpu.VMEM((1024, 512), BF16),
                pltpu.VMEM((1024, 1024), BF16),
                pltpu.VMEM((COLS, 512), BF16),
                pltpu.VMEM((COLS, 1024), BF16),
                pltpu.VMEM((COLS, 1024), BF16),
                pltpu.SemaphoreType.DMA((2,)),
            ],
            flops=2 * 805306368,
            moved=8 << 20,
            room=50500 << 10,
        )(table, near, far, *operators, couplings, factors)

    def to_owners(kept, given, width):
        got = other_core(given)
        (sent,) = call(
            parcels,
            "parcels",
            [out((64, PART, width), BF16)],
            [SMEM, SMEM, VMEM, VMEM, VMEM, VMEM],
            [pltpu.VMEM((BLOCKS, HALF, BI), F32)],
        )(table, table_far, kept, got, facts, base)
        return swap_all(sent, YXZ)

    paired, linked = neighbours(rhs)
    opened, held = call(
        opening,
        "opening",
        [out((GROUPS, 8, COLS), F32), out((ROWS, COLS), F32)],
        [SMEM, VMEM],
    )(halo_ids, rhs)
    facts = swap_all(opened, YX)
    precond_v, diag_v = call(
        bring_owned,
        "bring_owned",
        [out(precond.shape, BF16), out(schur_diag.shape, BF16)],
        [HBM, HBM],
        [pltpu.SemaphoreType.DMA((2,))],
    )(precond, schur_diag)
    operators = call(
        bring_slot,
        "bring_slot",
        [out((1024, 512), BF16), out((1024, 1024), BF16)],
        [HBM, HBM],
        [pltpu.SemaphoreType.DMA((2,))],
        room=52000 << 10,
    )(couplings, factors)
    sent, z_one, base, basis = call(
        first_direction,
        "first_direction",
        [
            out((GROUPS, HALF, ROWS), BF16),
            out((ROWS, COLS), F32),
            out((PART, ROWS), F32),
            out((PART, ROWS), F32),
        ],
        [SMEM, SMEM, VMEM, VMEM, VMEM, VMEM, VMEM, VMEM],
        [pltpu.VMEM((COLS, ROWS), F32)],
        flops=1 << 26,
    )(table, table_far, held, paired, linked, facts, precond_v, diag_v)
    near = swap_all(sent, YX)
    far = other_core(near)
    kept, given = apply_slots(near, far)
    arrived = to_owners(kept, given, 2 * ROWS)
    sent, base, w = call(
        second_direction,
        "second_direction",
        [out((64, PART, ROWS), BF16), out((PART, ROWS), F32), out((PART, ROWS), F32)],
        [VMEM, VMEM, VMEM, VMEM],
        flops=1 << 26,
    )(arrived, base, precond_v, diag_v)
    near = swap_all(sent, YXZ).reshape(GROUPS, HALF, ROWS)
    far = other_core(near)
    kept, given = apply_slots(near, far)
    arrived = to_owners(kept, given, ROWS)
    (sent,) = call(
        products, "products", [out((64, 8, COLS), F32)], [SMEM, VMEM, VMEM, VMEM, VMEM]
    )(table, arrived, base, w, basis)
    sums = swap_all(sent, YXZ)
    sums_far = other_core(sums)
    own = [lax.dynamic_slice_in_dim(half, partner(group), 1, 0) for half in (near, far)]
    (answer,) = call(
        closing, "closing", [out((ROWS, COLS), F32)], [SMEM] + [VMEM] * 6
    )(table, sums, sums_far, facts, z_one, *own)
    return answer


def solution(mesh):
    torus = Mesh(mesh.devices.reshape(4, 4, 4, 2), ALL)
    placed = (
        P(SUB, None),
        P(SUB, None),
        P(SUB, None),
        P(SUB, None),
        P(ALL, None, None),
        P(ALL, None, None),
        P(ALL, None),
        P(ALL),
    )
    return jax.shard_map(
        on_device, mesh=torus, in_specs=placed, out_specs=P(SUB, None), check_vma=False
    )
```

```python
import jax
import jax.numpy as jnp
from jax import lax
from jax.experimental import pallas as pl
from jax.experimental.pallas import tpu as pltpu
from jax.sharding import Mesh
from jax.sharding import PartitionSpec as P

BI = 128
ROWS = 256
COLS = 128
HALF = 64
PART = 16
GROUPS = 16
BLOCKS = 32
SUB = ("x", "y")
YX = ("y", "x")
YXZ = ("y", "x", "z")
ALL = ("x", "y", "z", "c")
F32 = jnp.float32
BF16 = jnp.bfloat16
SHRINK = 2.0**-31
VMEM = pl.BlockSpec(memory_space=pltpu.VMEM)
SMEM = pl.BlockSpec(memory_space=pltpu.SMEM)
ANY = pl.BlockSpec(memory_space=pl.ANY)
HBM = pl.BlockSpec(memory_space=pltpu.HBM)
GROUP, DEPTH, CORE, LIVE, HALO, IDS = 0, 1, 2, 3, 4, 6
NT = (((1,), (1,)), ((), ()))
NN = (((1,), (0,)), ((), ()))


def dot(left, right, dims=NN):
    return lax.dot_general(left, right, dims, preferred_element_type=F32)


def call(body, name, outs, specs, scratch=(), flops=0, moved=1 << 20, room=4 << 20):
    return pl.pallas_call(
        body,
        name=name,
        out_shape=outs,
        in_specs=specs,
        out_specs=[VMEM] * len(outs),
        scratch_shapes=list(scratch),
        cost_estimate=pl.CostEstimate(flops=flops, bytes_accessed=moved, transcendentals=0),
        compiler_params=pltpu.CompilerParams(vmem_limit_bytes=room),
    )


def out(shape, dtype):
    return jax.ShapeDtypeStruct(shape, dtype)


def partner(group):
    return ((group & 3) << 2) | (group >> 2)


def block_at(table, place):
    return pl.ds(pl.multiple_of((table[place] & 1) * BI, BI), BI)


def opening(halo, rhs, sent, held):
    field = rhs[...]
    held[...] = field
    sums = jnp.sum(field * field, axis=0, keepdims=True)
    row = lax.broadcasted_iota(jnp.int32, (8, COLS), 0)
    left = (halo[0, 0] & 1).astype(F32)
    right = (halo[0, 1] & 1).astype(F32)
    tile = jnp.where(row == 0, sums, jnp.where(row == 1, left, jnp.where(row == 2, right, 0.0)))
    sent[...] = jnp.broadcast_to(tile[None], sent.shape)


def bring_owned(precond, diag, precond_v, diag_v, sems):
    copies = [
        pltpu.make_async_copy(precond, precond_v, sems.at[0]),
        pltpu.make_async_copy(diag, diag_v, sems.at[1]),
    ]
    for copy in copies:
        copy.start()
    for copy in copies:
        copy.wait()


def bring_slots(table, couplings, factors, coup_a, coup_b, fact_a, fact_b, sems):
    def copies(slot, coup, fact):
        return (
            pltpu.make_async_copy(couplings.at[slot], coup, sems.at[slot, 0]),
            pltpu.make_async_copy(factors.at[slot], fact, sems.at[slot, 1]),
        )

    for copy in copies(0, coup_a, fact_a):
        copy.start()

    @pl.when(table[LIVE] > 1)
    def _():
        for copy in copies(1, coup_b, fact_b):
            copy.start()
        for copy in copies(1, coup_b, fact_b):
            copy.wait()

    for copy in copies(0, coup_a, fact_a):
        copy.wait()


def first_direction(
    table, table_far, rhs, paired, linked, facts, precond, diag, sent, z_nat, base, basis, turned
):
    beta = jnp.sqrt(jnp.sum(facts[:, 0:1, :], axis=0))
    v = rhs[...] / beta
    odd = (table[GROUP] & 1) == 1
    lower = block_at(table, HALO)
    upper = block_at(table, HALO + 1)
    left = jnp.where(odd, paired[lower, :], linked[lower, :]) / beta
    right = jnp.where(odd, linked[upper, :], paired[upper, :]) / beta
    patch = jnp.concatenate([v, left, right], axis=0).astype(BF16)
    z = v + dot(precond[...], patch)
    z_nat[...] = z
    half = pl.ds(pl.multiple_of(table[CORE] * HALF, HALF), HALF)
    part = pl.ds(pl.multiple_of(table[CORE] * HALF + table[DEPTH] * PART, PART), PART)
    turned[...] = z.T
    mine = turned[half, :].astype(BF16)
    sent[...] = jnp.broadcast_to(mine[None], sent.shape)
    turned[...] = (3.0 * z + dot(diag[...], z.astype(BF16))).T
    base[...] = turned[part, :]
    turned[...] = v.T
    basis[...] = turned[part, :]


def slots(
    table, near, far, coup_a, coup_b, fact_a, fact_b, kept, given, picked, one, two
):
    def slot(number, coup, fact):
        for j in range(4):
            block = table[IDS + number * 4 + j]
            place = partner(block >> 1)
            lanes = pl.ds(pl.multiple_of((block & 1) * BI, BI), BI)
            picked[0:HALF, j * BI : (j + 1) * BI] = near[place, :, lanes]
            picked[HALF:COLS, j * BI : (j + 1) * BI] = far[place, :, lanes]
        for n in range(4):
            span = slice(n * 256, (n + 1) * 256)
            one[:, span] = dot(picked[...], coup[span, :], NT).astype(BF16)
        for n in range(4):
            span = slice(n * 256, (n + 1) * 256)
            two[:, span] = dot(one[...], fact[span, :], NT).astype(BF16)
        for n in range(4):
            span = slice(n * 256, (n + 1) * 256)
            one[:, span] = dot(two[...], fact[:, span]).astype(BF16)
        for n in range(2):
            piece = dot(one[...], coup[:, n * 256 : (n + 1) * 256])
            for m in range(2):
                lanes = slice(m * BI, (m + 1) * BI)
                kept[number * 4 + n * 2 + m] = piece[0:HALF, lanes]
                given[number * 4 + n * 2 + m] = piece[HALF:COLS, lanes]

    slot(0, coup_a, fact_a)

    @pl.when(table[LIVE] > 1)
    def _():
        slot(1, coup_b, fact_b)

    @pl.when(table[LIVE] < 2)
    def _():
        kept[4:8] = jnp.zeros((4, HALF, BI), F32)
        given[4:8] = jnp.zeros((4, HALF, BI), F32)


def parcels(table, table_far, kept, got, facts, base, sent, total):
    total[...] = jnp.zeros_like(total)
    for i in range(8):
        block = table[IDS + i]
        total[block] = total[block] + kept[i]
    for i in range(8):
        block = table_far[IDS + i]
        total[block] = total[block] + got[i]
    with_halo = sent.shape[2] > ROWS

    def group(d, carry):
        place = partner(d)
        lower = 2 * ((d + GROUPS - 1) & (GROUPS - 1))
        upper = 2 * ((d + 1) & (GROUPS - 1))
        blocks = [total[2 * d], total[2 * d + 1]]
        if with_halo:
            left = facts[place, 1:2, :] > 0.5
            right = facts[place, 2:3, :] > 0.5
            blocks.append(jnp.where(left, total[lower + 1], total[lower]))
            blocks.append(jnp.where(right, total[upper + 1], total[upper]))
        for j, block in enumerate(blocks):
            low = block.astype(BF16)
            for z in range(4):
                sent[place * 4 + z, :, j * BI : (j + 1) * BI] = low[z * PART : (z + 1) * PART]
        return carry

    lax.fori_loop(0, GROUPS, group, 0)
    if with_halo:
        mine = table[GROUP]
        depth = table[DEPTH]
        part = pl.ds(pl.multiple_of(depth * PART, PART), PART)
        for side, other in ((0, mine + 1), (1, mine + GROUPS - 1)):
            other = partner(other & (GROUPS - 1))
            upper = facts[other, side + 1 : side + 2, :] > 0.5
            block = jnp.where(upper, total[2 * mine + 1, part, :], total[2 * mine, part, :])
            stays = jnp.where(upper, base[:, BI:], base[:, :BI])
            lanes = slice(ROWS + side * BI, ROWS + (side + 1) * BI)
            sent[other * 4 + depth, :, lanes] = (block - stays).astype(BF16)


def summed(arrived):
    def add(i, total):
        for j in range(8):
            total = total + arrived[i * 8 + j].astype(F32)
        return total

    return lax.fori_loop(0, 8, add, jnp.zeros(arrived.shape[1:], F32))


def second_direction(arrived, base, precond, diag, sent, base_two, w):
    coupled = summed(arrived)
    image = base[...] - coupled[:, :ROWS]
    patch = jnp.concatenate([image, -coupled[:, ROWS:]], axis=1).astype(BF16)
    z = image + dot(patch, precond[...], NT)
    low = z.astype(BF16)
    w[...] = image
    base_two[...] = 3.0 * z + dot(low, diag[...], NT)
    sent[...] = jnp.broadcast_to(low[None], sent.shape)


def products(table, arrived, base, w, basis, sent):
    image = (base[...] - summed(arrived)) * SHRINK
    one = w[...]
    v = basis[...]
    lane = lax.broadcasted_iota(jnp.int32, (PART, COLS), 1)
    row = lax.broadcasted_iota(jnp.int32, (PART, COLS), 0)
    here = lane == row + (table[CORE] * HALF + table[DEPTH] * PART)
    rank = lax.broadcasted_iota(jnp.int32, (8, COLS), 0)
    tile = jnp.zeros((8, COLS), F32)
    pairs = [(v, one), (one, one), (v, image), (one, image), (image, image)]
    for k, (left, right) in enumerate(pairs):
        value = jnp.sum(left * right, axis=1, keepdims=True)
        spread = jnp.sum(jnp.where(here, value, 0.0), axis=0, keepdims=True)
        tile = jnp.where(rank == k, spread, tile)
    sent[...] = jnp.broadcast_to(tile[None], sent.shape)


def closing(table, near, far, facts, z_one, z_near, z_far, answer):
    sums = jnp.sum(near[...], axis=0) + jnp.sum(far[...], axis=0)
    beta = jnp.sqrt(jnp.sum(facts[:, 0:1, :], axis=0))
    h11, ww, vx, wx, xx = (sums[k : k + 1] for k in range(5))
    h21 = jnp.sqrt(ww - h11 * h11)
    small = SHRINK * h11
    h12 = (vx - small * h11) / (SHRINK * h21)
    h22 = ((wx - h11 * vx) - small * ww + small * h11 * h11) / (SHRINK * h21) / h21
    scaled = SHRINK * h21
    norm = ((xx - 2.0 * small * wx) + small * small * ww) / scaled / scaled
    low_square = norm - h12 * h12 - h22 * h22
    rho = jnp.sqrt(h11 * h11 + h21 * h21)
    cosine = h11 / rho
    sine = h21 / rho
    top = cosine * h12 + sine * h22
    low = cosine * h22 - sine * h12
    y2 = -low * sine * beta / (low * low + low_square)
    y1 = (cosine * beta - top * y2) / rho
    second = y2 / h21
    first = y1 - second * h11
    a = z_near[0].astype(F32)
    b = z_far[0].astype(F32)
    swap = table[CORE] == 1
    stacked = jnp.concatenate([jnp.where(swap, b, a), jnp.where(swap, a, b)], axis=0)
    answer[...] = first * z_one[...] + second * stacked.T


def other_core(array):
    return lax.ppermute(array, "c", [(0, 1), (1, 0)])


def swap_all(array, axes):
    return lax.all_to_all(array, axes, split_axis=0, concat_axis=0, tiled=True)


def neighbours(array):
    paired = lax.ppermute(array, SUB, [(i, i ^ 1) for i in range(GROUPS)])
    linked = lax.ppermute(array, SUB, [(i, (i - 1 + 2 * (i & 1)) % GROUPS) for i in range(GROUPS)])
    return paired, linked


def on_device(rhs, schur_diag, precond, halo_ids, factors, couplings, block_ids, counts):
    group = lax.axis_index(SUB)
    place = jnp.stack([group, lax.axis_index("z"), lax.axis_index("c")]).astype(jnp.int32)
    table = jnp.concatenate([place, counts, halo_ids.reshape(-1), block_ids.reshape(-1)])
    table_far = other_core(table)

    def apply_slots(near, far):
        return call(
            slots,
            "slots",
            [out((8, HALF, BI), F32), out((8, HALF, BI), F32)],
            [SMEM] + [VMEM] * 6,
            [
                pltpu.VMEM((COLS, 512), BF16),
                pltpu.VMEM((COLS, 1024), BF16),
                pltpu.VMEM((COLS, 1024), BF16),
            ],
            flops=2 * 805306368,
            moved=8 << 20,
        )(table, near, far, *operators)

    def to_owners(kept, given, width):
        got = other_core(given)
        (sent,) = call(
            parcels,
            "parcels",
            [out((64, PART, width), BF16)],
            [SMEM, SMEM, VMEM, VMEM, VMEM, VMEM],
            [pltpu.VMEM((BLOCKS, HALF, BI), F32)],
        )(table, table_far, kept, got, facts, base)
        return swap_all(sent, YXZ)

    paired, linked = neighbours(rhs)
    opened, held = call(
        opening,
        "opening",
        [out((GROUPS, 8, COLS), F32), out((ROWS, COLS), F32)],
        [SMEM, VMEM],
    )(halo_ids, rhs)
    facts = swap_all(opened, YX)
    precond_v, diag_v = call(
        bring_owned,
        "bring_owned",
        [out(precond.shape, BF16), out(schur_diag.shape, BF16)],
        [HBM, HBM],
        [pltpu.SemaphoreType.DMA((2,))],
    )(precond, schur_diag)
    operators = call(
        bring_slots,
        "bring_slots",
        [out((1024, 512), BF16)] * 2 + [out((1024, 1024), BF16)] * 2,
        [SMEM, HBM, HBM],
        [pltpu.SemaphoreType.DMA((2, 2))],
        room=46000 << 10,
    )(table, couplings, factors)
    sent, z_one, base, basis = call(
        first_direction,
        "first_direction",
        [
            out((GROUPS, HALF, ROWS), BF16),
            out((ROWS, COLS), F32),
            out((PART, ROWS), F32),
            out((PART, ROWS), F32),
        ],
        [SMEM, SMEM, VMEM, VMEM, VMEM, VMEM, VMEM, VMEM],
        [pltpu.VMEM((COLS, ROWS), F32)],
        flops=1 << 26,
    )(table, table_far, held, paired, linked, facts, precond_v, diag_v)
    near = swap_all(sent, YX)
    far = other_core(near)
    kept, given = apply_slots(near, far)
    arrived = to_owners(kept, given, 2 * ROWS)
    sent, base, w = call(
        second_direction,
        "second_direction",
        [out((64, PART, ROWS), BF16), out((PART, ROWS), F32), out((PART, ROWS), F32)],
        [VMEM, VMEM, VMEM, VMEM],
        flops=1 << 26,
    )(arrived, base, precond_v, diag_v)
    near = swap_all(sent, YXZ).reshape(GROUPS, HALF, ROWS)
    far = other_core(near)
    kept, given = apply_slots(near, far)
    arrived = to_owners(kept, given, ROWS)
    (sent,) = call(
        products, "products", [out((64, 8, COLS), F32)], [SMEM, VMEM, VMEM, VMEM, VMEM]
    )(table, arrived, base, w, basis)
    sums = swap_all(sent, YXZ)
    sums_far = other_core(sums)
    own = [lax.dynamic_slice_in_dim(half, partner(group), 1, 0) for half in (near, far)]
    (answer,) = call(
        closing, "closing", [out((ROWS, COLS), F32)], [SMEM] + [VMEM] * 6
    )(table, sums, sums_far, facts, z_one, *own)
    return answer


def solution(mesh):
    torus = Mesh(mesh.devices.reshape(4, 4, 4, 2), ALL)
    placed = (
        P(SUB, None),
        P(SUB, None),
        P(SUB, None),
        P(SUB, None),
        P(ALL, None, None),
        P(ALL, None, None),
        P(ALL, None),
        P(ALL),
    )
    return jax.shard_map(
        on_device, mesh=torus, in_specs=placed, out_specs=P(SUB, None), check_vma=False
    )
```

```python
import jax
import jax.numpy as jnp
from jax import lax
from jax.experimental import pallas as pl
from jax.experimental.pallas import tpu as pltpu
from jax.sharding import Mesh
from jax.sharding import PartitionSpec as P

BI = 128
ROWS = 256
COLS = 128
HALF = 64
PART = 16
GROUPS = 16
BLOCKS = 32
SUB = ("x", "y")
YX = ("y", "x")
YXZ = ("y", "x", "z")
ALL = ("x", "y", "z", "c")
F32 = jnp.float32
BF16 = jnp.bfloat16
SHRINK = 2.0**-31
VMEM = pl.BlockSpec(memory_space=pltpu.VMEM)
SMEM = pl.BlockSpec(memory_space=pltpu.SMEM)
ANY = pl.BlockSpec(memory_space=pl.ANY)
HBM = pl.BlockSpec(memory_space=pltpu.HBM)
GROUP, DEPTH, CORE, LIVE, HALO, IDS = 0, 1, 2, 3, 4, 6
NT = (((1,), (1,)), ((), ()))
NN = (((1,), (0,)), ((), ()))


def dot(left, right, dims=NN):
    return lax.dot_general(left, right, dims, preferred_element_type=F32)


def call(body, outs, specs, scratch=(), flops=0, moved=1 << 20, room=4 << 20):
    return pl.pallas_call(
        body,
        out_shape=outs,
        in_specs=specs,
        out_specs=[VMEM] * len(outs),
        scratch_shapes=list(scratch),
        cost_estimate=pl.CostEstimate(flops=flops, bytes_accessed=moved, transcendentals=0),
        compiler_params=pltpu.CompilerParams(vmem_limit_bytes=room),
    )


def out(shape, dtype):
    return jax.ShapeDtypeStruct(shape, dtype)


def partner(group):
    return ((group & 3) << 2) | (group >> 2)


def block_at(table, place):
    return pl.ds(pl.multiple_of((table[place] & 1) * BI, BI), BI)


def opening(halo, rhs, sent, held):
    field = rhs[...]
    held[...] = field
    sums = jnp.sum(field * field, axis=0, keepdims=True)
    row = lax.broadcasted_iota(jnp.int32, (8, COLS), 0)
    left = (halo[0, 0] & 1).astype(F32)
    right = (halo[0, 1] & 1).astype(F32)
    tile = jnp.where(row == 0, sums, jnp.where(row == 1, left, jnp.where(row == 2, right, 0.0)))
    sent[...] = jnp.broadcast_to(tile[None], sent.shape)


def bring_owned(precond, diag, precond_v, diag_v, sems):
    copies = [
        pltpu.make_async_copy(precond, precond_v, sems.at[0]),
        pltpu.make_async_copy(diag, diag_v, sems.at[1]),
    ]
    for copy in copies:
        copy.start()
    for copy in copies:
        copy.wait()


def bring_slots(table, couplings, factors, coup_a, coup_b, fact_a, fact_b, sems):
    def copies(slot, coup, fact):
        return (
            pltpu.make_async_copy(couplings.at[slot], coup, sems.at[slot, 0]),
            pltpu.make_async_copy(factors.at[slot], fact, sems.at[slot, 1]),
        )

    for copy in copies(0, coup_a, fact_a):
        copy.start()

    @pl.when(table[LIVE] > 1)
    def _():
        for copy in copies(1, coup_b, fact_b):
            copy.start()
        for copy in copies(1, coup_b, fact_b):
            copy.wait()

    for copy in copies(0, coup_a, fact_a):
        copy.wait()


def first_direction(
    table, table_far, rhs, own, other, facts, precond, diag, sent, z_nat, base, basis, turned
):
    beta = jnp.sqrt(jnp.sum(facts[:, 0:1, :], axis=0))
    v = rhs[...] / beta
    lower = block_at(table, HALO)
    upper = block_at(table, HALO + 1)
    flip = ((table[GROUP] + table[CORE]) & 1) == 1
    left = jnp.where(flip, own[lower, :], other[lower, :]) / beta
    right = jnp.where(flip, other[upper, :], own[upper, :]) / beta
    patch = jnp.concatenate([v, left, right], axis=0).astype(BF16)
    z = v + dot(precond[...], patch)
    z_nat[...] = z
    half = pl.ds(pl.multiple_of(table[CORE] * HALF, HALF), HALF)
    part = pl.ds(pl.multiple_of(table[CORE] * HALF + table[DEPTH] * PART, PART), PART)
    turned[...] = z.T
    mine = turned[half, :].astype(BF16)
    sent[...] = jnp.broadcast_to(mine[None], sent.shape)
    turned[...] = (3.0 * z + dot(diag[...], z.astype(BF16))).T
    base[...] = turned[part, :]
    turned[...] = v.T
    basis[...] = turned[part, :]


def slots(
    table, near, far, coup_a, coup_b, fact_a, fact_b, kept, given, picked, one, two
):
    def slot(number, coup, fact):
        for j in range(4):
            block = table[IDS + number * 4 + j]
            place = partner(block >> 1)
            lanes = pl.ds(pl.multiple_of((block & 1) * BI, BI), BI)
            picked[0:HALF, j * BI : (j + 1) * BI] = near[place, :, lanes]
            picked[HALF:COLS, j * BI : (j + 1) * BI] = far[place, :, lanes]
        for n in range(4):
            span = slice(n * 256, (n + 1) * 256)
            one[:, span] = dot(picked[...], coup[span, :], NT).astype(BF16)
        for n in range(4):
            span = slice(n * 256, (n + 1) * 256)
            two[:, span] = dot(one[...], fact[span, :], NT).astype(BF16)
        for n in range(4):
            span = slice(n * 256, (n + 1) * 256)
            one[:, span] = dot(two[...], fact[:, span]).astype(BF16)
        for n in range(2):
            piece = dot(one[...], coup[:, n * 256 : (n + 1) * 256])
            for m in range(2):
                lanes = slice(m * BI, (m + 1) * BI)
                kept[number * 4 + n * 2 + m] = piece[0:HALF, lanes]
                given[number * 4 + n * 2 + m] = piece[HALF:COLS, lanes]

    slot(0, coup_a, fact_a)

    @pl.when(table[LIVE] > 1)
    def _():
        slot(1, coup_b, fact_b)

    @pl.when(table[LIVE] < 2)
    def _():
        kept[4:8] = jnp.zeros((4, HALF, BI), F32)
        given[4:8] = jnp.zeros((4, HALF, BI), F32)


def parcels(table, table_far, kept, got, facts, base, sent, total):
    total[...] = jnp.zeros_like(total)
    for i in range(8):
        block = table[IDS + i]
        total[block] = total[block] + kept[i]
    for i in range(8):
        block = table_far[IDS + i]
        total[block] = total[block] + got[i]
    with_halo = sent.shape[2] > ROWS

    def group(d, carry):
        place = partner(d)
        lower = 2 * ((d + GROUPS - 1) & (GROUPS - 1))
        upper = 2 * ((d + 1) & (GROUPS - 1))
        blocks = [total[2 * d], total[2 * d + 1]]
        if with_halo:
            left = facts[place, 1:2, :] > 0.5
            right = facts[place, 2:3, :] > 0.5
            blocks.append(jnp.where(left, total[lower + 1], total[lower]))
            blocks.append(jnp.where(right, total[upper + 1], total[upper]))
        for j, block in enumerate(blocks):
            low = block.astype(BF16)
            for z in range(4):
                sent[place * 4 + z, :, j * BI : (j + 1) * BI] = low[z * PART : (z + 1) * PART]
        return carry

    lax.fori_loop(0, GROUPS, group, 0)
    if with_halo:
        mine = table[GROUP]
        depth = table[DEPTH]
        part = pl.ds(pl.multiple_of(depth * PART, PART), PART)
        for side, other in ((0, mine + 1), (1, mine + GROUPS - 1)):
            other = partner(other & (GROUPS - 1))
            upper = facts[other, side + 1 : side + 2, :] > 0.5
            block = jnp.where(upper, total[2 * mine + 1, part, :], total[2 * mine, part, :])
            stays = jnp.where(upper, base[:, BI:], base[:, :BI])
            lanes = slice(ROWS + side * BI, ROWS + (side + 1) * BI)
            sent[other * 4 + depth, :, lanes] = (block - stays).astype(BF16)


def summed(arrived):
    def add(i, total):
        for j in range(8):
            total = total + arrived[i * 8 + j].astype(F32)
        return total

    return lax.fori_loop(0, 8, add, jnp.zeros(arrived.shape[1:], F32))


def second_direction(arrived, base, precond, diag, sent, base_two, w):
    coupled = summed(arrived)
    image = base[...] - coupled[:, :ROWS]
    patch = jnp.concatenate([image, -coupled[:, ROWS:]], axis=1).astype(BF16)
    z = image + dot(patch, precond[...], NT)
    low = z.astype(BF16)
    w[...] = image
    base_two[...] = 3.0 * z + dot(low, diag[...], NT)
    sent[...] = jnp.broadcast_to(low[None], sent.shape)


def products(table, arrived, base, w, basis, sent):
    image = (base[...] - summed(arrived)) * SHRINK
    one = w[...]
    v = basis[...]
    lane = lax.broadcasted_iota(jnp.int32, (PART, COLS), 1)
    row = lax.broadcasted_iota(jnp.int32, (PART, COLS), 0)
    here = lane == row + (table[CORE] * HALF + table[DEPTH] * PART)
    rank = lax.broadcasted_iota(jnp.int32, (8, COLS), 0)
    tile = jnp.zeros((8, COLS), F32)
    pairs = [(v, one), (one, one), (v, image), (one, image), (image, image)]
    for k, (left, right) in enumerate(pairs):
        value = jnp.sum(left * right, axis=1, keepdims=True)
        spread = jnp.sum(jnp.where(here, value, 0.0), axis=0, keepdims=True)
        tile = jnp.where(rank == k, spread, tile)
    sent[...] = jnp.broadcast_to(tile[None], sent.shape)


def closing(table, near, far, facts, z_one, z_near, z_far, answer):
    sums = jnp.sum(near[...], axis=0) + jnp.sum(far[...], axis=0)
    beta = jnp.sqrt(jnp.sum(facts[:, 0:1, :], axis=0))
    h11, ww, vx, wx, xx = (sums[k : k + 1] for k in range(5))
    h21 = jnp.sqrt(ww - h11 * h11)
    small = SHRINK * h11
    h12 = (vx - small * h11) / (SHRINK * h21)
    h22 = ((wx - h11 * vx) - small * ww + small * h11 * h11) / (SHRINK * h21) / h21
    scaled = SHRINK * h21
    norm = ((xx - 2.0 * small * wx) + small * small * ww) / scaled / scaled
    low_square = norm - h12 * h12 - h22 * h22
    rho = jnp.sqrt(h11 * h11 + h21 * h21)
    cosine = h11 / rho
    sine = h21 / rho
    top = cosine * h12 + sine * h22
    low = cosine * h22 - sine * h12
    y2 = -low * sine * beta / (low * low + low_square)
    y1 = (cosine * beta - top * y2) / rho
    second = y2 / h21
    first = y1 - second * h11
    a = z_near[0].astype(F32)
    b = z_far[0].astype(F32)
    swap = table[CORE] == 1
    stacked = jnp.concatenate([jnp.where(swap, b, a), jnp.where(swap, a, b)], axis=0)
    answer[...] = first * z_one[...] + second * stacked.T


def other_core(array):
    return lax.ppermute(array, "c", [(0, 1), (1, 0)])


def swap_all(array, axes):
    return lax.all_to_all(array, axes, split_axis=0, concat_axis=0, tiled=True)


def one_neighbour(array):
    pairs = []
    for i in range(GROUPS):
        pairs.append((2 * i, 2 * (i ^ 1)))
        pairs.append((2 * i + 1, 2 * ((i - 1 + 2 * (i & 1)) % GROUPS) + 1))
    return lax.ppermute(array, ("x", "y", "c"), pairs)


def on_device(rhs, schur_diag, precond, halo_ids, factors, couplings, block_ids, counts):
    group = lax.axis_index(SUB)
    place = jnp.stack([group, lax.axis_index("z"), lax.axis_index("c")]).astype(jnp.int32)
    table = jnp.concatenate([place, counts, halo_ids.reshape(-1), block_ids.reshape(-1)])
    table_far = other_core(table)

    def apply_slots(near, far):
        return call(
            slots,
            [out((8, HALF, BI), F32), out((8, HALF, BI), F32)],
            [SMEM] + [VMEM] * 6,
            [
                pltpu.VMEM((COLS, 512), BF16),
                pltpu.VMEM((COLS, 1024), BF16),
                pltpu.VMEM((COLS, 1024), BF16),
            ],
            flops=2 * 805306368,
            moved=8 << 20,
        )(table, near, far, *operators)

    def to_owners(kept, given, width):
        got = other_core(given)
        (sent,) = call(
            parcels,
            [out((64, PART, width), BF16)],
            [SMEM, SMEM, VMEM, VMEM, VMEM, VMEM],
            [pltpu.VMEM((BLOCKS, HALF, BI), F32)],
        )(table, table_far, kept, got, facts, base)
        return swap_all(sent, YXZ)

    own = one_neighbour(rhs)
    other = other_core(own)
    opened, held = call(
        opening, [out((GROUPS, 8, COLS), F32), out((ROWS, COLS), F32)], [SMEM, VMEM]
    )(halo_ids, rhs)
    facts = swap_all(opened, YX)
    precond_v, diag_v = call(
        bring_owned,
        [out(precond.shape, BF16), out(schur_diag.shape, BF16)],
        [HBM, HBM],
        [pltpu.SemaphoreType.DMA((2,))],
    )(precond, schur_diag)
    operators = call(
        bring_slots,
        [out((1024, 512), BF16)] * 2 + [out((1024, 1024), BF16)] * 2,
        [SMEM, HBM, HBM],
        [pltpu.SemaphoreType.DMA((2, 2))],
        room=46000 << 10,
    )(table, couplings, factors)
    sent, z_one, base, basis = call(
        first_direction,
        [
            out((GROUPS, HALF, ROWS), BF16),
            out((ROWS, COLS), F32),
            out((PART, ROWS), F32),
            out((PART, ROWS), F32),
        ],
        [SMEM, SMEM, VMEM, VMEM, VMEM, VMEM, VMEM, VMEM],
        [pltpu.VMEM((COLS, ROWS), F32)],
        flops=1 << 26,
    )(table, table_far, held, own, other, facts, precond_v, diag_v)
    near = swap_all(sent, YX)
    far = other_core(near)
    kept, given = apply_slots(near, far)
    arrived = to_owners(kept, given, 2 * ROWS)
    sent, base, w = call(
        second_direction,
        [out((64, PART, ROWS), BF16), out((PART, ROWS), F32), out((PART, ROWS), F32)],
        [VMEM, VMEM, VMEM, VMEM],
        flops=1 << 26,
    )(arrived, base, precond_v, diag_v)
    near = swap_all(sent, YXZ).reshape(GROUPS, HALF, ROWS)
    far = other_core(near)
    kept, given = apply_slots(near, far)
    arrived = to_owners(kept, given, ROWS)
    (sent,) = call(
        products, [out((64, 8, COLS), F32)], [SMEM, VMEM, VMEM, VMEM, VMEM]
    )(table, arrived, base, w, basis)
    sums = swap_all(sent, YXZ)
    sums_far = other_core(sums)
    own = [lax.dynamic_slice_in_dim(half, partner(group), 1, 0) for half in (near, far)]
    (answer,) = call(
        closing, [out((ROWS, COLS), F32)], [SMEM] + [VMEM] * 6
    )(table, sums, sums_far, facts, z_one, *own)
    return answer


def solution(mesh):
    torus = Mesh(mesh.devices.reshape(4, 4, 4, 2), ALL)
    placed = (
        P(SUB, None),
        P(SUB, None),
        P(SUB, None),
        P(SUB, None),
        P(ALL, None, None),
        P(ALL, None, None),
        P(ALL, None),
        P(ALL),
    )

    return jax.shard_map(
        on_device, mesh=torus, in_specs=placed, out_specs=P(SUB, None), check_vma=False
    )
```

```python
import jax
import jax.numpy as jnp
from jax import lax
from jax.experimental import pallas as pl
from jax.experimental.pallas import tpu as pltpu
from jax.sharding import Mesh
from jax.sharding import PartitionSpec as P

BI = 128
ROWS = 256
COLS = 128
HALF = 64
PART = 16
GROUPS = 16
BLOCKS = 32
SUB = ("x", "y")
YX = ("y", "x")
YXZ = ("y", "x", "z")
ALL = ("x", "y", "z", "c")
F32 = jnp.float32
BF16 = jnp.bfloat16
SHRINK = 2.0**-31
VMEM = pl.BlockSpec(memory_space=pltpu.VMEM)
SMEM = pl.BlockSpec(memory_space=pltpu.SMEM)
ANY = pl.BlockSpec(memory_space=pl.ANY)
HBM = pl.BlockSpec(memory_space=pltpu.HBM)
GROUP, DEPTH, CORE, LIVE, HALO, IDS = 0, 1, 2, 3, 4, 6
NT = (((1,), (1,)), ((), ()))
NN = (((1,), (0,)), ((), ()))


def dot(left, right, dims=NN):
    return lax.dot_general(left, right, dims, preferred_element_type=F32)


def call(body, outs, specs, scratch=(), flops=0, moved=1 << 20, room=4 << 20):
    return pl.pallas_call(
        body,
        out_shape=outs,
        in_specs=specs,
        out_specs=[VMEM] * len(outs),
        scratch_shapes=list(scratch),
        cost_estimate=pl.CostEstimate(flops=flops, bytes_accessed=moved, transcendentals=0),
        compiler_params=pltpu.CompilerParams(vmem_limit_bytes=room),
    )


def out(shape, dtype):
    return jax.ShapeDtypeStruct(shape, dtype)


def partner(group):
    return ((group & 3) << 2) | (group >> 2)


def block_at(table, place):
    return pl.ds(pl.multiple_of((table[place] & 1) * BI, BI), BI)


def opening(halo, rhs, sent, held, sem):
    copy = pltpu.make_async_copy(rhs, held, sem)
    copy.start()
    copy.wait()
    field = held[...]
    sums = jnp.sum(field * field, axis=0, keepdims=True)
    row = lax.broadcasted_iota(jnp.int32, (8, COLS), 0)
    left = (halo[0, 0] & 1).astype(F32)
    right = (halo[0, 1] & 1).astype(F32)
    tile = jnp.where(row == 0, sums, jnp.where(row == 1, left, jnp.where(row == 2, right, 0.0)))
    sent[...] = jnp.broadcast_to(tile[None], sent.shape)


def bring_owned(precond, diag, precond_v, diag_v, sems):
    copies = [
        pltpu.make_async_copy(precond, precond_v, sems.at[0]),
        pltpu.make_async_copy(diag, diag_v, sems.at[1]),
    ]
    for copy in copies:
        copy.start()
    for copy in copies:
        copy.wait()


def bring_slots(table, couplings, factors, coup_a, coup_b, fact_a, fact_b, sems):
    def copies(slot, coup, fact):
        return (
            pltpu.make_async_copy(couplings.at[slot], coup, sems.at[slot, 0]),
            pltpu.make_async_copy(factors.at[slot], fact, sems.at[slot, 1]),
        )

    for copy in copies(0, coup_a, fact_a):
        copy.start()

    @pl.when(table[LIVE] > 1)
    def _():
        for copy in copies(1, coup_b, fact_b):
            copy.start()
        for copy in copies(1, coup_b, fact_b):
            copy.wait()

    for copy in copies(0, coup_a, fact_a):
        copy.wait()


def first_direction(
    table, table_far, rhs, own, other, facts, precond, diag, sent, z_nat, base, basis, turned
):
    beta = jnp.sqrt(jnp.sum(facts[:, 0:1, :], axis=0))
    v = rhs[...] / beta
    lower = block_at(table, HALO)
    upper = block_at(table, HALO + 1)
    flip = ((table[GROUP] + table[CORE]) & 1) == 1
    left = jnp.where(flip, own[lower, :], other[lower, :]) / beta
    right = jnp.where(flip, other[upper, :], own[upper, :]) / beta
    patch = jnp.concatenate([v, left, right], axis=0).astype(BF16)
    z = v + dot(precond[...], patch)
    z_nat[...] = z
    half = pl.ds(pl.multiple_of(table[CORE] * HALF, HALF), HALF)
    part = pl.ds(pl.multiple_of(table[CORE] * HALF + table[DEPTH] * PART, PART), PART)
    turned[...] = z.T
    mine = turned[half, :].astype(BF16)
    sent[...] = jnp.broadcast_to(mine[None], sent.shape)
    turned[...] = (3.0 * z + dot(diag[...], z.astype(BF16))).T
    base[...] = turned[part, :]
    turned[...] = v.T
    basis[...] = turned[part, :]


def slots(
    table, near, far, coup_a, coup_b, fact_a, fact_b, kept, given, picked, one, two
):
    def slot(number, coup, fact):
        for j in range(4):
            block = table[IDS + number * 4 + j]
            place = partner(block >> 1)
            lanes = pl.ds(pl.multiple_of((block & 1) * BI, BI), BI)
            picked[0:HALF, j * BI : (j + 1) * BI] = near[place, :, lanes]
            picked[HALF:COLS, j * BI : (j + 1) * BI] = far[place, :, lanes]
        for n in range(4):
            span = slice(n * 256, (n + 1) * 256)
            one[:, span] = dot(picked[...], coup[span, :], NT).astype(BF16)
        for n in range(4):
            span = slice(n * 256, (n + 1) * 256)
            two[:, span] = dot(one[...], fact[span, :], NT).astype(BF16)
        for n in range(4):
            span = slice(n * 256, (n + 1) * 256)
            one[:, span] = dot(two[...], fact[:, span]).astype(BF16)
        for n in range(2):
            piece = dot(one[...], coup[:, n * 256 : (n + 1) * 256])
            for m in range(2):
                lanes = slice(m * BI, (m + 1) * BI)
                kept[number * 4 + n * 2 + m] = piece[0:HALF, lanes]
                given[number * 4 + n * 2 + m] = piece[HALF:COLS, lanes]

    slot(0, coup_a, fact_a)

    @pl.when(table[LIVE] > 1)
    def _():
        slot(1, coup_b, fact_b)

    @pl.when(table[LIVE] < 2)
    def _():
        kept[4:8] = jnp.zeros((4, HALF, BI), F32)
        given[4:8] = jnp.zeros((4, HALF, BI), F32)


def parcels(table, table_far, kept, got, facts, base, sent, total):
    total[...] = jnp.zeros_like(total)
    for i in range(8):
        block = table[IDS + i]
        total[block] = total[block] + kept[i]
    for i in range(8):
        block = table_far[IDS + i]
        total[block] = total[block] + got[i]
    with_halo = sent.shape[2] > ROWS

    def group(d, carry):
        place = partner(d)
        lower = 2 * ((d + GROUPS - 1) & (GROUPS - 1))
        upper = 2 * ((d + 1) & (GROUPS - 1))
        blocks = [total[2 * d], total[2 * d + 1]]
        if with_halo:
            left = facts[place, 1:2, :] > 0.5
            right = facts[place, 2:3, :] > 0.5
            blocks.append(jnp.where(left, total[lower + 1], total[lower]))
            blocks.append(jnp.where(right, total[upper + 1], total[upper]))
        for j, block in enumerate(blocks):
            low = block.astype(BF16)
            for z in range(4):
                sent[place * 4 + z, :, j * BI : (j + 1) * BI] = low[z * PART : (z + 1) * PART]
        return carry

    lax.fori_loop(0, GROUPS, group, 0)
    if with_halo:
        mine = table[GROUP]
        depth = table[DEPTH]
        part = pl.ds(pl.multiple_of(depth * PART, PART), PART)
        for side, other in ((0, mine + 1), (1, mine + GROUPS - 1)):
            other = partner(other & (GROUPS - 1))
            upper = facts[other, side + 1 : side + 2, :] > 0.5
            block = jnp.where(upper, total[2 * mine + 1, part, :], total[2 * mine, part, :])
            stays = jnp.where(upper, base[:, BI:], base[:, :BI])
            lanes = slice(ROWS + side * BI, ROWS + (side + 1) * BI)
            sent[other * 4 + depth, :, lanes] = (block - stays).astype(BF16)


def summed(arrived):
    def add(i, total):
        for j in range(8):
            total = total + arrived[i * 8 + j].astype(F32)
        return total

    return lax.fori_loop(0, 8, add, jnp.zeros(arrived.shape[1:], F32))


def second_direction(arrived, base, precond, diag, sent, base_two, w):
    coupled = summed(arrived)
    image = base[...] - coupled[:, :ROWS]
    patch = jnp.concatenate([image, -coupled[:, ROWS:]], axis=1).astype(BF16)
    z = image + dot(patch, precond[...], NT)
    low = z.astype(BF16)
    w[...] = image
    base_two[...] = 3.0 * z + dot(low, diag[...], NT)
    sent[...] = jnp.broadcast_to(low[None], sent.shape)


def products(table, arrived, base, w, basis, sent):
    image = (base[...] - summed(arrived)) * SHRINK
    one = w[...]
    v = basis[...]
    lane = lax.broadcasted_iota(jnp.int32, (PART, COLS), 1)
    row = lax.broadcasted_iota(jnp.int32, (PART, COLS), 0)
    here = lane == row + (table[CORE] * HALF + table[DEPTH] * PART)
    rank = lax.broadcasted_iota(jnp.int32, (8, COLS), 0)
    tile = jnp.zeros((8, COLS), F32)
    pairs = [(v, one), (one, one), (v, image), (one, image), (image, image)]
    for k, (left, right) in enumerate(pairs):
        value = jnp.sum(left * right, axis=1, keepdims=True)
        spread = jnp.sum(jnp.where(here, value, 0.0), axis=0, keepdims=True)
        tile = jnp.where(rank == k, spread, tile)
    sent[...] = jnp.broadcast_to(tile[None], sent.shape)


def closing(table, near, far, facts, z_one, z_near, z_far, answer):
    sums = jnp.sum(near[...], axis=0) + jnp.sum(far[...], axis=0)
    beta = jnp.sqrt(jnp.sum(facts[:, 0:1, :], axis=0))
    h11, ww, vx, wx, xx = (sums[k : k + 1] for k in range(5))
    h21 = jnp.sqrt(ww - h11 * h11)
    small = SHRINK * h11
    h12 = (vx - small * h11) / (SHRINK * h21)
    h22 = ((wx - h11 * vx) - small * ww + small * h11 * h11) / (SHRINK * h21) / h21
    scaled = SHRINK * h21
    norm = ((xx - 2.0 * small * wx) + small * small * ww) / scaled / scaled
    low_square = norm - h12 * h12 - h22 * h22
    rho = jnp.sqrt(h11 * h11 + h21 * h21)
    cosine = h11 / rho
    sine = h21 / rho
    top = cosine * h12 + sine * h22
    low = cosine * h22 - sine * h12
    y2 = -low * sine * beta / (low * low + low_square)
    y1 = (cosine * beta - top * y2) / rho
    second = y2 / h21
    first = y1 - second * h11
    a = z_near[0].astype(F32)
    b = z_far[0].astype(F32)
    swap = table[CORE] == 1
    stacked = jnp.concatenate([jnp.where(swap, b, a), jnp.where(swap, a, b)], axis=0)
    answer[...] = first * z_one[...] + second * stacked.T


def other_core(array):
    return lax.ppermute(array, "c", [(0, 1), (1, 0)])


def swap_all(array, axes):
    return lax.all_to_all(array, axes, split_axis=0, concat_axis=0, tiled=True)


def one_neighbour(array):
    pairs = []
    for i in range(GROUPS):
        pairs.append((2 * i, 2 * (i ^ 1)))
        pairs.append((2 * i + 1, 2 * ((i - 1 + 2 * (i & 1)) % GROUPS) + 1))
    return lax.ppermute(array, ("x", "y", "c"), pairs)


def on_device(rhs, schur_diag, precond, halo_ids, factors, couplings, block_ids, counts):
    group = lax.axis_index(SUB)
    place = jnp.stack([group, lax.axis_index("z"), lax.axis_index("c")]).astype(jnp.int32)
    table = jnp.concatenate([place, counts, halo_ids.reshape(-1), block_ids.reshape(-1)])
    table_far = other_core(table)

    def apply_slots(near, far):
        return call(
            slots,
            [out((8, HALF, BI), F32), out((8, HALF, BI), F32)],
            [SMEM] + [VMEM] * 6,
            [
                pltpu.VMEM((COLS, 512), BF16),
                pltpu.VMEM((COLS, 1024), BF16),
                pltpu.VMEM((COLS, 1024), BF16),
            ],
            flops=2 * 805306368,
            moved=8 << 20,
        )(table, near, far, *operators)

    def to_owners(kept, given, width):
        got = other_core(given)
        (sent,) = call(
            parcels,
            [out((64, PART, width), BF16)],
            [SMEM, SMEM, VMEM, VMEM, VMEM, VMEM],
            [pltpu.VMEM((BLOCKS, HALF, BI), F32)],
        )(table, table_far, kept, got, facts, base)
        return swap_all(sent, YXZ)

    own = one_neighbour(rhs)
    other = other_core(own)
    opened, held = call(
        opening,
        [out((GROUPS, 8, COLS), F32), out((ROWS, COLS), F32)],
        [SMEM, HBM],
        [pltpu.SemaphoreType.DMA],
        room=55000 << 10,
    )(halo_ids, rhs)
    facts = swap_all(opened, YX)
    precond_v, diag_v = call(
        bring_owned,
        [out(precond.shape, BF16), out(schur_diag.shape, BF16)],
        [HBM, HBM],
        [pltpu.SemaphoreType.DMA((2,))],
    )(precond, schur_diag)
    operators = call(
        bring_slots,
        [out((1024, 512), BF16)] * 2 + [out((1024, 1024), BF16)] * 2,
        [SMEM, HBM, HBM],
        [pltpu.SemaphoreType.DMA((2, 2))],
        room=46000 << 10,
    )(table, couplings, factors)
    sent, z_one, base, basis = call(
        first_direction,
        [
            out((GROUPS, HALF, ROWS), BF16),
            out((ROWS, COLS), F32),
            out((PART, ROWS), F32),
            out((PART, ROWS), F32),
        ],
        [SMEM, SMEM, VMEM, VMEM, VMEM, VMEM, VMEM, VMEM],
        [pltpu.VMEM((COLS, ROWS), F32)],
        flops=1 << 26,
    )(table, table_far, held, own, other, facts, precond_v, diag_v)
    near = swap_all(sent, YX)
    far = other_core(near)
    kept, given = apply_slots(near, far)
    arrived = to_owners(kept, given, 2 * ROWS)
    sent, base, w = call(
        second_direction,
        [out((64, PART, ROWS), BF16), out((PART, ROWS), F32), out((PART, ROWS), F32)],
        [VMEM, VMEM, VMEM, VMEM],
        flops=1 << 26,
    )(arrived, base, precond_v, diag_v)
    near = swap_all(sent, YXZ).reshape(GROUPS, HALF, ROWS)
    far = other_core(near)
    kept, given = apply_slots(near, far)
    arrived = to_owners(kept, given, ROWS)
    (sent,) = call(
        products, [out((64, 8, COLS), F32)], [SMEM, VMEM, VMEM, VMEM, VMEM]
    )(table, arrived, base, w, basis)
    sums = swap_all(sent, YXZ)
    sums_far = other_core(sums)
    own = [lax.dynamic_slice_in_dim(half, partner(group), 1, 0) for half in (near, far)]
    (answer,) = call(
        closing, [out((ROWS, COLS), F32)], [SMEM] + [VMEM] * 6
    )(table, sums, sums_far, facts, z_one, *own)
    return answer


def solution(mesh):
    torus = Mesh(mesh.devices.reshape(4, 4, 4, 2), ALL)
    placed = (
        P(SUB, None),
        P(SUB, None),
        P(SUB, None),
        P(SUB, None),
        P(ALL, None, None),
        P(ALL, None, None),
        P(ALL, None),
        P(ALL),
    )

    return jax.shard_map(
        on_device, mesh=torus, in_specs=placed, out_specs=P(SUB, None), check_vma=False
    )
```

```python
import jax
import jax.numpy as jnp
from jax import lax
from jax.experimental import pallas as pl
from jax.experimental.pallas import tpu as pltpu
from jax.sharding import Mesh
from jax.sharding import PartitionSpec as P

BI = 128
ROWS = 256
COLS = 128
HALF = 64
PART = 16
GROUPS = 16
BLOCKS = 32
SUB = ("x", "y")
YX = ("y", "x")
YXZ = ("y", "x", "z")
ALL = ("x", "y", "z", "c")
F32 = jnp.float32
BF16 = jnp.bfloat16
SHRINK = 2.0**-31
VMEM = pl.BlockSpec(memory_space=pltpu.VMEM)
SMEM = pl.BlockSpec(memory_space=pltpu.SMEM)
ANY = pl.BlockSpec(memory_space=pl.ANY)
HBM = pl.BlockSpec(memory_space=pltpu.HBM)
GROUP, DEPTH, CORE, LIVE, HALO, IDS = 0, 1, 2, 3, 4, 6
NT = (((1,), (1,)), ((), ()))
NN = (((1,), (0,)), ((), ()))


def dot(left, right, dims=NN):
    return lax.dot_general(left, right, dims, preferred_element_type=F32)


def call(body, outs, specs, scratch=(), flops=0, moved=1 << 20, room=4 << 20):
    return pl.pallas_call(
        body,
        out_shape=outs,
        in_specs=specs,
        out_specs=[VMEM] * len(outs),
        scratch_shapes=list(scratch),
        cost_estimate=pl.CostEstimate(flops=flops, bytes_accessed=moved, transcendentals=0),
        compiler_params=pltpu.CompilerParams(vmem_limit_bytes=room),
    )


def out(shape, dtype):
    return jax.ShapeDtypeStruct(shape, dtype)


def partner(group):
    return ((group & 3) << 2) | (group >> 2)


def block_at(table, place):
    return pl.ds(pl.multiple_of((table[place] & 1) * BI, BI), BI)


def opening(halo, rhs, sent, held):
    field = rhs[...]
    held[...] = field
    sums = jnp.sum(field * field, axis=0, keepdims=True)
    row = lax.broadcasted_iota(jnp.int32, (8, COLS), 0)
    left = (halo[0, 0] & 1).astype(F32)
    right = (halo[0, 1] & 1).astype(F32)
    tile = jnp.where(row == 0, sums, jnp.where(row == 1, left, jnp.where(row == 2, right, 0.0)))
    sent[...] = jnp.broadcast_to(tile[None], sent.shape)


def bring_owned(precond, diag, precond_v, diag_v, sems):
    copies = [
        pltpu.make_async_copy(precond, precond_v, sems.at[0]),
        pltpu.make_async_copy(diag, diag_v, sems.at[1]),
    ]
    for copy in copies:
        copy.start()
    for copy in copies:
        copy.wait()


def bring_slots(table, couplings, factors, coup_a, coup_b, fact_a, fact_b, sems):
    def copies(slot, coup, fact):
        return (
            pltpu.make_async_copy(couplings.at[slot], coup, sems.at[slot, 0]),
            pltpu.make_async_copy(factors.at[slot], fact, sems.at[slot, 1]),
        )

    for copy in copies(0, coup_a, fact_a):
        copy.start()

    @pl.when(table[LIVE] > 1)
    def _():
        for copy in copies(1, coup_b, fact_b):
            copy.start()
        for copy in copies(1, coup_b, fact_b):
            copy.wait()

    for copy in copies(0, coup_a, fact_a):
        copy.wait()


def first_direction(
    table, table_far, rhs, own, other, facts, precond, diag, sent, z_nat, base, basis, turned
):
    beta = jnp.sqrt(jnp.sum(facts[:, 0:1, :], axis=0))
    v = rhs[...] / beta
    lower = block_at(table, HALO)
    upper = block_at(table, HALO + 1)
    flip = ((table[GROUP] + table[CORE]) & 1) == 1
    left = jnp.where(flip, own[lower, :], other[lower, :]) / beta
    right = jnp.where(flip, other[upper, :], own[upper, :]) / beta
    patch = jnp.concatenate([v, left, right], axis=0).astype(BF16)
    z = v + dot(precond[...], patch)
    z_nat[...] = z
    half = pl.ds(pl.multiple_of(table[CORE] * HALF, HALF), HALF)
    part = pl.ds(pl.multiple_of(table[CORE] * HALF + table[DEPTH] * PART, PART), PART)
    turned[...] = z.T
    mine = turned[half, :].astype(BF16)
    sent[...] = jnp.broadcast_to(mine[None], sent.shape)
    turned[...] = (3.0 * z + dot(diag[...], z.astype(BF16))).T
    base[...] = turned[part, :]
    turned[...] = v.T
    basis[...] = turned[part, :]


def slots(
    table, near, far, coup_a, coup_b, fact_a, fact_b, kept, given, picked, one, two
):
    def slot(number, coup, fact):
        for j in range(4):
            block = table[IDS + number * 4 + j]
            place = partner(block >> 1)
            lanes = pl.ds(pl.multiple_of((block & 1) * BI, BI), BI)
            picked[0:HALF, j * BI : (j + 1) * BI] = near[place, :, lanes]
            picked[HALF:COLS, j * BI : (j + 1) * BI] = far[place, :, lanes]
        for n in range(4):
            span = slice(n * 256, (n + 1) * 256)
            one[:, span] = dot(picked[...], coup[span, :], NT).astype(BF16)
        for n in range(4):
            span = slice(n * 256, (n + 1) * 256)
            two[:, span] = dot(one[...], fact[span, :], NT).astype(BF16)
        for n in range(4):
            span = slice(n * 256, (n + 1) * 256)
            one[:, span] = dot(two[...], fact[:, span]).astype(BF16)
        for n in range(2):
            piece = dot(one[...], coup[:, n * 256 : (n + 1) * 256])
            for m in range(2):
                lanes = slice(m * BI, (m + 1) * BI)
                kept[number * 4 + n * 2 + m] = piece[0:HALF, lanes]
                given[number * 4 + n * 2 + m] = piece[HALF:COLS, lanes].astype(BF16)

    slot(0, coup_a, fact_a)

    @pl.when(table[LIVE] > 1)
    def _():
        slot(1, coup_b, fact_b)

    @pl.when(table[LIVE] < 2)
    def _():
        kept[4:8] = jnp.zeros((4, HALF, BI), F32)
        given[4:8] = jnp.zeros((4, HALF, BI), BF16)


def parcels(table, table_far, kept, got, facts, base, sent, total):
    total[...] = jnp.zeros_like(total)
    for i in range(8):
        block = table[IDS + i]
        total[block] = total[block] + kept[i]
    for i in range(8):
        block = table_far[IDS + i]
        total[block] = total[block] + got[i].astype(F32)
    with_halo = sent.shape[2] > ROWS

    def group(d, carry):
        place = partner(d)
        lower = 2 * ((d + GROUPS - 1) & (GROUPS - 1))
        upper = 2 * ((d + 1) & (GROUPS - 1))
        blocks = [total[2 * d], total[2 * d + 1]]
        if with_halo:
            left = facts[place, 1:2, :] > 0.5
            right = facts[place, 2:3, :] > 0.5
            blocks.append(jnp.where(left, total[lower + 1], total[lower]))
            blocks.append(jnp.where(right, total[upper + 1], total[upper]))
        for j, block in enumerate(blocks):
            low = block.astype(BF16)
            for z in range(4):
                sent[place * 4 + z, :, j * BI : (j + 1) * BI] = low[z * PART : (z + 1) * PART]
        return carry

    lax.fori_loop(0, GROUPS, group, 0)
    if with_halo:
        mine = table[GROUP]
        depth = table[DEPTH]
        part = pl.ds(pl.multiple_of(depth * PART, PART), PART)
        for side, other in ((0, mine + 1), (1, mine + GROUPS - 1)):
            other = partner(other & (GROUPS - 1))
            upper = facts[other, side + 1 : side + 2, :] > 0.5
            block = jnp.where(upper, total[2 * mine + 1, part, :], total[2 * mine, part, :])
            stays = jnp.where(upper, base[:, BI:], base[:, :BI])
            lanes = slice(ROWS + side * BI, ROWS + (side + 1) * BI)
            sent[other * 4 + depth, :, lanes] = (block - stays).astype(BF16)


def summed(arrived):
    def add(i, total):
        for j in range(8):
            total = total + arrived[i * 8 + j].astype(F32)
        return total

    return lax.fori_loop(0, 8, add, jnp.zeros(arrived.shape[1:], F32))


def second_direction(arrived, base, precond, diag, sent, base_two, w):
    coupled = summed(arrived)
    image = base[...] - coupled[:, :ROWS]
    patch = jnp.concatenate([image, -coupled[:, ROWS:]], axis=1).astype(BF16)
    z = image + dot(patch, precond[...], NT)
    low = z.astype(BF16)
    w[...] = image
    base_two[...] = 3.0 * z + dot(low, diag[...], NT)
    sent[...] = jnp.broadcast_to(low[None], sent.shape)


def products(table, arrived, base, w, basis, sent):
    image = (base[...] - summed(arrived)) * SHRINK
    one = w[...]
    v = basis[...]
    lane = lax.broadcasted_iota(jnp.int32, (PART, COLS), 1)
    row = lax.broadcasted_iota(jnp.int32, (PART, COLS), 0)
    here = lane == row + (table[CORE] * HALF + table[DEPTH] * PART)
    rank = lax.broadcasted_iota(jnp.int32, (8, COLS), 0)
    tile = jnp.zeros((8, COLS), F32)
    pairs = [(v, one), (one, one), (v, image), (one, image), (image, image)]
    for k, (left, right) in enumerate(pairs):
        value = jnp.sum(left * right, axis=1, keepdims=True)
        spread = jnp.sum(jnp.where(here, value, 0.0), axis=0, keepdims=True)
        tile = jnp.where(rank == k, spread, tile)
    sent[...] = jnp.broadcast_to(tile[None], sent.shape)


def closing(table, near, far, facts, z_one, z_near, z_far, answer):
    sums = jnp.sum(near[...], axis=0) + jnp.sum(far[...], axis=0)
    beta = jnp.sqrt(jnp.sum(facts[:, 0:1, :], axis=0))
    h11, ww, vx, wx, xx = (sums[k : k + 1] for k in range(5))
    h21 = jnp.sqrt(ww - h11 * h11)
    small = SHRINK * h11
    h12 = (vx - small * h11) / (SHRINK * h21)
    h22 = ((wx - h11 * vx) - small * ww + small * h11 * h11) / (SHRINK * h21) / h21
    scaled = SHRINK * h21
    norm = ((xx - 2.0 * small * wx) + small * small * ww) / scaled / scaled
    low_square = norm - h12 * h12 - h22 * h22
    rho = jnp.sqrt(h11 * h11 + h21 * h21)
    cosine = h11 / rho
    sine = h21 / rho
    top = cosine * h12 + sine * h22
    low = cosine * h22 - sine * h12
    y2 = -low * sine * beta / (low * low + low_square)
    y1 = (cosine * beta - top * y2) / rho
    second = y2 / h21
    first = y1 - second * h11
    a = z_near[0].astype(F32)
    b = z_far[0].astype(F32)
    swap = table[CORE] == 1
    stacked = jnp.concatenate([jnp.where(swap, b, a), jnp.where(swap, a, b)], axis=0)
    answer[...] = first * z_one[...] + second * stacked.T


def other_core(array):
    return lax.ppermute(array, "c", [(0, 1), (1, 0)])


def swap_all(array, axes):
    return lax.all_to_all(array, axes, split_axis=0, concat_axis=0, tiled=True)


def one_neighbour(array):
    pairs = []
    for i in range(GROUPS):
        pairs.append((2 * i, 2 * (i ^ 1)))
        pairs.append((2 * i + 1, 2 * ((i - 1 + 2 * (i & 1)) % GROUPS) + 1))
    return lax.ppermute(array, ("x", "y", "c"), pairs)


def on_device(rhs, schur_diag, precond, halo_ids, factors, couplings, block_ids, counts):
    group = lax.axis_index(SUB)
    place = jnp.stack([group, lax.axis_index("z"), lax.axis_index("c")]).astype(jnp.int32)
    table = jnp.concatenate([place, counts, halo_ids.reshape(-1), block_ids.reshape(-1)])
    table_far = other_core(table)

    def apply_slots(near, far):
        return call(
            slots,
            [out((8, HALF, BI), F32), out((8, HALF, BI), BF16)],
            [SMEM] + [VMEM] * 6,
            [
                pltpu.VMEM((COLS, 512), BF16),
                pltpu.VMEM((COLS, 1024), BF16),
                pltpu.VMEM((COLS, 1024), BF16),
            ],
            flops=2 * 805306368,
            moved=8 << 20,
        )(table, near, far, *operators)

    def to_owners(kept, given, width):
        got = other_core(given)
        (sent,) = call(
            parcels,
            [out((64, PART, width), BF16)],
            [SMEM, SMEM, VMEM, VMEM, VMEM, VMEM],
            [pltpu.VMEM((BLOCKS, HALF, BI), F32)],
        )(table, table_far, kept, got, facts, base)
        return swap_all(sent, YXZ)

    own = one_neighbour(rhs)
    other = other_core(own)
    opened, held = call(
        opening, [out((GROUPS, 8, COLS), F32), out((ROWS, COLS), F32)], [SMEM, VMEM]
    )(halo_ids, rhs)
    facts = swap_all(opened, YX)
    precond_v, diag_v = call(
        bring_owned,
        [out(precond.shape, BF16), out(schur_diag.shape, BF16)],
        [HBM, HBM],
        [pltpu.SemaphoreType.DMA((2,))],
    )(precond, schur_diag)
    operators = call(
        bring_slots,
        [out((1024, 512), BF16)] * 2 + [out((1024, 1024), BF16)] * 2,
        [SMEM, HBM, HBM],
        [pltpu.SemaphoreType.DMA((2, 2))],
        room=46000 << 10,
    )(table, couplings, factors)
    sent, z_one, base, basis = call(
        first_direction,
        [
            out((GROUPS, HALF, ROWS), BF16),
            out((ROWS, COLS), F32),
            out((PART, ROWS), F32),
            out((PART, ROWS), F32),
        ],
        [SMEM, SMEM, VMEM, VMEM, VMEM, VMEM, VMEM, VMEM],
        [pltpu.VMEM((COLS, ROWS), F32)],
        flops=1 << 26,
    )(table, table_far, held, own, other, facts, precond_v, diag_v)
    near = swap_all(sent, YX)
    far = other_core(near)
    kept, given = apply_slots(near, far)
    arrived = to_owners(kept, given, 2 * ROWS)
    sent, base, w = call(
        second_direction,
        [out((64, PART, ROWS), BF16), out((PART, ROWS), F32), out((PART, ROWS), F32)],
        [VMEM, VMEM, VMEM, VMEM],
        flops=1 << 26,
    )(arrived, base, precond_v, diag_v)
    near = swap_all(sent, YXZ).reshape(GROUPS, HALF, ROWS)
    far = other_core(near)
    kept, given = apply_slots(near, far)
    arrived = to_owners(kept, given, ROWS)
    (sent,) = call(
        products, [out((64, 8, COLS), F32)], [SMEM, VMEM, VMEM, VMEM, VMEM]
    )(table, arrived, base, w, basis)
    sums = swap_all(sent, YXZ)
    sums_far = other_core(sums)
    own = [lax.dynamic_slice_in_dim(half, partner(group), 1, 0) for half in (near, far)]
    (answer,) = call(
        closing, [out((ROWS, COLS), F32)], [SMEM] + [VMEM] * 6
    )(table, sums, sums_far, facts, z_one, *own)
    return answer


def solution(mesh):
    torus = Mesh(mesh.devices.reshape(4, 4, 4, 2), ALL)
    placed = (
        P(SUB, None),
        P(SUB, None),
        P(SUB, None),
        P(SUB, None),
        P(ALL, None, None),
        P(ALL, None, None),
        P(ALL, None),
        P(ALL),
    )

    return jax.shard_map(
        on_device, mesh=torus, in_specs=placed, out_specs=P(SUB, None), check_vma=False
    )
```
